512 devices in a mesh: mem: 8 (over z_hi, core), grid: 64 (over y, x, z_lo).
Axes of the slice: x: 4, y: 8, z: 8 (z_hi: 4, z_lo: 2; z = z_hi * 2 + z_lo), core: 2. Of those that a mesh axis runs over, the one named last changes fastest.
Arguments:
- control: bfloat16 [32, 32, 384, 768], P('mem', None, 'grid'), may hold values from -6 to 6
- perturbation: bfloat16 [32, 32, 768, 384], P('mem', None, 'grid'), may hold values from -6 to 6
- vertical: bfloat16 [32, 32], replicated, may hold values from 0 to 1
- lat_counts: int32 [64], replicated, may hold values from 1 to 6, 361 in all
- lon_counts: int32 [64], replicated, may hold values from 1 to 12, 720 in all
Outputs:
- increment: float32 [32, 768, 384], P('mem', 'grid')
The draws below stay inside these ranges and needn't reach their ends.
Inputs may be any that keep to these rules, and one draw needn't show every extreme that they name: Slab g holds its first lat_counts[g] latitude slots as real rows, numbered on from the slabs before it. Slab g holds its first lon_counts[g] longitude slots as real columns, numbered on from the slabs before it.
All inputs are finite; a program needn't handle non-finite values.
Results may differ from the reference program's by a relative error of at most 0.0067.
Values may be sent and summed in bfloat16 or wider, within the bound.
A program may use at most 64 MiB of HBM per device.

```python
import math
import jax
import jax.numpy as jnp
import numpy as np
from jax import lax

LAT = 361
LON = 720
LEV = 32
LENGTH = 8
BAND = 48
MEMBERS = 32
LAT_SLOT = 6
LON_SLOT = 12
LAT_PAD = 384
LON_PAD = 768
N_GRID = 64


def draw_vertical(key, part):
    level_index = jnp.arange(LEV).astype(jnp.float32)
    decay_base = jnp.exp(-jnp.abs(level_index[:, None] - level_index[None, :]) / 4.0)
    factor = jax.random.uniform(key, (LEV, LEV), jnp.float32, 0.5, 1.5)
    return (decay_base * factor / 3.0).astype(jnp.bfloat16)


def raised(array, own_key, source, target, shards_of, factor):
    owner, partner = [(jnp.arange(array.shape[dim]) // (array.shape[dim] // shards_of)).reshape([-1 if axis == dim else 1 for axis in range(array.ndim)]) for dim in (source, target)]
    chosen = jax.random.permutation(own_key, shards_of)[partner]
    strong = (owner == chosen) | (owner == (partner + shards_of // 2) % shards_of)
    return jnp.where(strong, factor * array, array)


def steps_of(key, dims, pieces, smallest, largest):
    level, own = 1.0, jax.random.fold_in(key, 6)
    for dim, blocks in pieces:
        draws = jnp.exp(jax.random.uniform(jax.random.fold_in(own, dim), (blocks,), jnp.float32, smallest / len(pieces), largest / len(pieces)))
        level = level * jnp.repeat(draws, dims[dim] // blocks).reshape([-1 if axis == dim else 1 for axis in range(len(dims))])
    return level


def profile(amount, total, reach, slope):
    loads = [(1 << 20) // math.isqrt(grade ** slope) + 1 for grade in range(2, amount + 1)]
    surplus, given = total - reach - (amount - 1), [1] * (amount - 1)
    while surplus > 0:
        movable = [i for i in range(amount - 1) if given[i] < reach]
        whole, remaining = sum([loads[i] for i in movable]), surplus
        for i in movable:
            more = min(reach - given[i], max(1, remaining * loads[i] // whole), surplus)
            given[i] = given[i] + more
            surplus = surplus - more
    return np.array([reach] + given)


def uneven(key, count, total, most, lean):
    if count == 2:
        one = jax.random.randint(key, (), max(1, total - most), min(most, total - 1) + 1)
        return jnp.stack([one, total - one])
    tallies = jnp.asarray(profile(count, total, most, lean), jnp.int32)
    couples = (count - 1) // 2
    source_of, receiver = tallies[1:1 + 2 * couples:2], tallies[2:2 + 2 * couples:2]
    margin = jnp.minimum(source_of - 1, most - receiver)
    shifted = jax.random.randint(jax.random.fold_in(key, 1), (couples,), 0, 1 << 20) % (margin + 1)
    tallies = tallies.at[1:1 + 2 * couples:2].set(source_of - shifted).at[2:2 + 2 * couples:2].set(receiver + shifted)
    return tallies[jax.random.permutation(jax.random.fold_in(key, 2), count)]


def bell_draw(stream_key, shape, width, limit, pieces=(), held_as=jnp.bfloat16):
    factor_of = steps_of(stream_key, shape, pieces, -0.22, 0.18) if pieces else 1.0
    entries = jax.random.normal(stream_key, shape, jnp.float32) * width * factor_of
    return jnp.minimum(jnp.maximum(entries, -limit), limit).astype(held_as)


def gaussian_with(own_key, shape, scale, reach, shards, heavy, held_as=jnp.bfloat16):
    values = scale * jax.random.normal(own_key, shape, jnp.float32)
    if shards:
        values = values * steps_of(own_key, shape, shards, -0.22, 0.18)
    return jnp.clip(raised(values, jax.random.fold_in(own_key, 3), *heavy), -reach, reach).astype(held_as)


def setup_inputs(seed: int = 0) -> dict:
    streams_of = jax.random.split(jax.random.key(seed), 6)
    return {
        "control": bell_draw(streams_of[0], (MEMBERS, LEV, LAT_PAD, LON_PAD), 1.0, 6.0, ((0, 8), (2, 64))),
        "perturbation": gaussian_with(streams_of[1], (MEMBERS, LEV, LON_PAD, LAT_PAD), 1.0, 6.0, ((0, 8), (2, 64)), (0, 1, 8, 2.0)),
        "vertical": draw_vertical(jax.random.fold_in(streams_of[5], 71), 0),
        "lat_counts": uneven(streams_of[3], N_GRID, LAT, LAT_SLOT, 2).astype(jnp.int32),
        "lon_counts": uneven(streams_of[4], N_GRID, LON, LON_SLOT, 2).astype(jnp.int32),
    }


def slot_table(counts, slot_count):
    devices = counts.shape[0]
    slot_ids = jnp.arange(devices * slot_count, dtype=jnp.int32)
    device_of = slot_ids // slot_count
    offset_in = slot_ids - device_of * slot_count
    offsets = (jnp.cumsum(counts) - counts).astype(jnp.int32)
    one_hot = device_of[:, None] == jnp.arange(devices, dtype=jnp.int32)[None, :]
    count_of = lax.optimization_barrier(jnp.sum(jnp.where(one_hot, counts[None, :], 0), axis=1)).astype(jnp.int32)
    start_of = lax.optimization_barrier(jnp.sum(jnp.where(one_hot, offsets[None, :], 0), axis=1)).astype(jnp.int32)
    return ((start_of + offset_in).astype(jnp.int32), offset_in < count_of)

def pass_matrix(counts, slot_count, extent, periodic):
    position, usable = slot_table(counts, slot_count)
    lag = (position[None, :] - position[:, None]).astype(jnp.int32)
    if periodic:
        lag = jnp.where(lag < 0, lag + extent, lag).astype(jnp.int32)
    steps_f = jnp.arange(0, BAND + 1).astype(jnp.float32)
    normal_sum = jnp.sqrt(jnp.sum(jnp.exp(-2.0 * steps_f / LENGTH)))
    lag_f = lag.astype(jnp.float32)
    inside = (lag >= 0) & (lag <= BAND) & usable[:, None] & usable[None, :]
    weight = jnp.where(inside, jnp.exp(-lag_f / LENGTH) / normal_sum, 0.0)
    return weight.astype(jnp.bfloat16)

def reference(control, perturbation, vertical, lat_counts, lon_counts):
    lon_matrix = pass_matrix(lon_counts, LON_SLOT, LON, True)
    lat_matrix = pass_matrix(lat_counts, LAT_SLOT, LAT, False)
    vertical_f = vertical.astype(jnp.float32)

    def member_step(running, member_pair):
        ctrl_member, pert_member = member_pair
        smooth = jnp.dot(ctrl_member.reshape(-1, LON_PAD), lon_matrix, preferred_element_type=jnp.float32)
        smooth = smooth.astype(jnp.bfloat16).reshape(LEV, LAT_PAD, LON_PAD)
        smooth = jnp.swapaxes(smooth, 1, 2)
        smooth = jnp.dot(smooth.reshape(-1, LAT_PAD), lat_matrix, preferred_element_type=jnp.float32)
        smooth = smooth.astype(jnp.bfloat16).reshape(LEV, LON_PAD, LAT_PAD)
        mixed = jnp.einsum('kl,lci->kci', vertical_f, smooth.astype(jnp.float32))
        return (running + mixed * pert_member.astype(jnp.float32), None)
    start = jnp.zeros((LEV, LON_PAD, LAT_PAD), jnp.float32)
    summed, unused = lax.scan(member_step, start, (control, perturbation))
    return summed
```

```python
import math

import jax
import jax.numpy as jnp
import numpy as np
from jax import lax
from jax.experimental import pallas as pl
from jax.experimental.pallas import tpu as pltpu
from jax.sharding import PartitionSpec as P

LAT = 361
LON = 720
LENGTH = 8
BAND = 48
MESH = pl.DeviceIdType.MESH
FAR = 20000.0
NORM = np.sqrt(np.sum(np.exp(np.float32(-2.0) * np.arange(BAND + 1, dtype=np.float32) / np.float32(LENGTH)), dtype=np.float32))
SCALE = float(np.float32(1.0) / NORM)

GRID = 64
MEM = 8
MEMBERS = 4
LEV = 32
ROWS = 6
COLS = 12
LON_PAD = GRID * COLS
LAT_PAD = GRID * ROWS
LANES = MEMBERS * LEV
CHUNK = 4
CHUNKS = COLS // CHUNK
PAIRS = ROWS // 2
BLOCK = CHUNK * ROWS
SHARE = LEV // MEM


def nt(a, b):
    return lax.dot_general(a, b, (((1,), (1,)), ((), ())), preferred_element_type=jnp.float32)


def iota(shape, dim):
    return lax.broadcasted_iota(jnp.int32, shape, dim)


def positions_down(counts, slab, place, missing):
    rows = slab.shape[0]
    devices = iota((rows, GRID), 1)
    table = jnp.broadcast_to(counts, (128, GRID)).astype(jnp.bfloat16)
    start = nt((devices < slab).astype(jnp.float32).astype(jnp.bfloat16), table)
    count = nt((devices == slab).astype(jnp.float32).astype(jnp.bfloat16), table)
    place = place.astype(jnp.float32)
    return jnp.where(place < count, start + place, missing)


def positions_across(counts, slab, place, missing):
    lanes = slab.shape[1]
    devices = iota((GRID, lanes), 0)
    table = jnp.broadcast_to(counts, (8, GRID)).astype(jnp.bfloat16)
    before = (devices < slab).astype(jnp.float32).astype(jnp.bfloat16)
    own = (devices == slab).astype(jnp.float32).astype(jnp.bfloat16)
    start = jnp.dot(table, before, preferred_element_type=jnp.float32)
    count = jnp.dot(table, own, preferred_element_type=jnp.float32)
    place = place.astype(jnp.float32)
    return jnp.where(place < count, start + place, missing)


def weights(lag, inside):
    return jnp.where(inside, jnp.exp(lag * (-1.0 / LENGTH)) * SCALE, 0.0).astype(jnp.bfloat16)


def interleave(first, second):
    low = iota(first.shape, 1) < 4
    even = jnp.where(low, first, pltpu.roll(second, 4, 1))
    odd = jnp.where(low, pltpu.roll(first, 4, 1), second)
    return even, odd


def kernel(control, perturbation, vertical, lat_counts, lon_counts, out,
           ctrl, pert, vert, latc, lonc, lon_t, lat_k, send, recv, wide, part, parts,
           in_sem, send_sem, recv_sem, own_sem, psend_sem, precv_sem, pown_sem):
    me = lax.axis_index("grid")
    mine = lax.axis_index("mem")
    loads = [pltpu.make_async_copy(source, target, in_sem.at[index]) for index, (source, target) in enumerate(
        ((lon_counts, lonc), (lat_counts, latc), (vertical, vert), (control, ctrl), (perturbation, pert)))]
    for load in loads:
        load.start()

    barrier = pltpu.get_barrier_semaphore()

    def greet(step, carry):
        pl.semaphore_signal(barrier, inc=1, device_id={"grid": lax.rem(me + step, GRID)}, device_id_type=MESH)
        return carry

    lax.fori_loop(1, GRID, greet, 0)
    for step in range(1, MEM):
        pl.semaphore_signal(barrier, inc=1, device_id={"mem": lax.rem(mine + step, MEM)}, device_id_type=MESH)

    loads[0].wait()
    counts = lonc[...].astype(jnp.float32)
    lanes = iota((GRID, LON_PAD), 1)
    source = positions_across(counts, lanes // COLS, lanes[:8] % COLS, -FAR)
    for q in range(CHUNKS):
        rows = iota((GRID * CHUNK, GRID), 0)
        place = iota((GRID * CHUNK, 128), 0) % CHUNK + q * CHUNK
        target = positions_down(counts, rows // CHUNK, place, FAR)
        for tile in range(LON_PAD // 128):
            lag = target - source[:1, tile * 128:(tile + 1) * 128]
            lag = jnp.where(lag < 0, lag + LON, lag)
            lon_t[q, :, tile * 128:(tile + 1) * 128] = weights(lag, lag <= BAND)

    loads[3].wait()
    own = []
    for q in range(CHUNKS):
        fields = jnp.concatenate([ctrl[:, i].reshape(LANES, LON_PAD) for i in range(ROWS)], axis=0)
        smooth = nt(lon_t[q], fields)
        for pair in range(PAIRS):
            first, second = [smooth[:, (2 * pair + half) * LANES:(2 * pair + half + 1) * LANES].reshape(GRID * CHUNK // 8, 8, LANES)
                             for half in range(2)]
            even, odd = interleave(first, second)
            send[q, :, 0, pair * 8:(pair + 1) * 8, :] = even.astype(jnp.bfloat16)
            send[q, :, 1, pair * 8:(pair + 1) * 8, :] = odd.astype(jnp.bfloat16)
        if q == 0:
            pl.semaphore_wait(barrier, GRID - 1 + MEM - 1)

        def push(step, carry):
            peer = lax.rem(me + step, GRID)
            pltpu.make_async_remote_copy(
                src_ref=send.at[q, peer // 2, peer % 2], dst_ref=recv.at[q, me],
                send_sem=send_sem.at[q], recv_sem=recv_sem.at[q],
                device_id={"grid": peer}, device_id_type=MESH).start()
            return carry

        lax.fori_loop(1, GRID, push, 0)
        keep = pltpu.make_async_copy(send.at[q, me // 2, me % 2], recv.at[q, me], own_sem.at[q])
        keep.start()
        own.append(keep)

    loads[1].wait()
    counts = latc[...].astype(jnp.float32)
    half_rows = GRID * PAIRS
    lanes = iota((GRID, LAT_PAD), 1)
    target = positions_across(counts, lanes // ROWS, lanes[:8] % ROWS, -FAR)
    rows = iota((LAT_PAD, GRID), 0) % half_rows
    long_rows = iota((LAT_PAD, 128), 0)
    place = 2 * (long_rows % PAIRS) + long_rows // half_rows
    source = positions_down(counts, rows // PAIRS, place, FAR)
    for tile in range(LAT_PAD // 128):
        lag = target[:1, tile * 128:(tile + 1) * 128] - source
        lat_k[:, tile * 128:(tile + 1) * 128] = weights(lag, (lag >= 0) & (lag <= BAND))

    loads[2].wait()
    spread = (iota((LEV, LANES), 0) == iota((LEV, LANES), 1) % LEV).astype(jnp.float32).astype(jnp.bfloat16)
    across = jnp.dot(vert[...], spread, preferred_element_type=jnp.float32)
    across = jnp.concatenate([across] * MEMBERS, axis=0)
    mixing = jnp.where(iota((LANES, LANES), 0) // LEV == iota((LANES, LANES), 1) // LEV, across, 0.0).astype(jnp.bfloat16)

    loads[4].wait()
    for q in range(CHUNKS):
        own[q].wait()
        pltpu.make_async_copy(recv.at[q, pl.ds(0, GRID - 1)], recv.at[q, pl.ds(0, GRID - 1)], recv_sem.at[q]).wait()
        wide[...] = recv[q].astype(jnp.float32).reshape(GRID * BLOCK, LANES)
        mixed = []
        for c in range(CHUNK):
            fields = jnp.concatenate([wide[pl.ds(half * CHUNK + c, half_rows, stride=2 * CHUNK), :] for half in range(2)], axis=0)
            mixed.append(nt(mixing, fields.astype(jnp.bfloat16)).astype(jnp.bfloat16))
        filtered = jnp.dot(jnp.concatenate(mixed, axis=0), lat_k[...], preferred_element_type=jnp.float32)
        sums = []
        for c in range(CHUNK):
            field = filtered[c * LANES:(c + 1) * LANES].reshape(MEMBERS, LEV, LAT_PAD)
            sums.append(jnp.sum(field * pert[:, q * CHUNK + c].astype(jnp.float32), axis=0).reshape(LEV // 8, 8, LAT_PAD))
        for two in range(CHUNK // 2):
            even, odd = interleave(sums[2 * two], sums[2 * two + 1])
            part[q, :, 0, two * 8:(two + 1) * 8, :] = even.astype(jnp.bfloat16)
            part[q, :, 1, two * 8:(two + 1) * 8, :] = odd.astype(jnp.bfloat16)
        for step in range(1, MEM):
            peer = lax.rem(mine + step, MEM)
            pltpu.make_async_remote_copy(
                src_ref=part.at[q, peer // 2, peer % 2], dst_ref=parts.at[q, mine],
                send_sem=psend_sem.at[q], recv_sem=precv_sem.at[q],
                device_id={"mem": peer}, device_id_type=MESH).start()
        pltpu.make_async_copy(part.at[q, mine // 2, mine % 2], parts.at[q, mine], pown_sem.at[q]).start()

    rows = CHUNK * SHARE
    for q in range(CHUNKS):
        pltpu.make_async_copy(part.at[q, 0, 0], parts.at[q, 0], pown_sem.at[q]).wait()
        pltpu.make_async_copy(parts.at[q, pl.ds(0, MEM - 1)], parts.at[q, pl.ds(0, MEM - 1)], precv_sem.at[q]).wait()
        out[q * rows:(q + 1) * rows, :] = jnp.sum(parts[q].astype(jnp.float32), axis=0)
    for q in range(CHUNKS):
        pltpu.make_async_copy(recv.at[q, pl.ds(0, GRID - 1)], recv.at[q, pl.ds(0, GRID - 1)], send_sem.at[q]).wait()
        pltpu.make_async_copy(parts.at[q, pl.ds(0, MEM - 1)], parts.at[q, pl.ds(0, MEM - 1)], psend_sem.at[q]).wait()


def per_device(control, perturbation, vertical, lat_counts, lon_counts):
    bf16 = jnp.bfloat16
    dma = pltpu.SemaphoreType.DMA
    rows = CHUNK * SHARE
    summed = pl.pallas_call(
        kernel,
        out_shape=jax.ShapeDtypeStruct((COLS * SHARE, LAT_PAD), jnp.float32),
        in_specs=[pl.BlockSpec(memory_space=pltpu.HBM)] * 5,
        out_specs=pl.BlockSpec(memory_space=pltpu.VMEM),
        scratch_shapes=[
            pltpu.VMEM((MEMBERS, ROWS, LEV, LON_PAD), bf16),
            pltpu.VMEM((MEMBERS, COLS, LEV, LAT_PAD), bf16),
            pltpu.VMEM((LEV, LEV), bf16),
            pltpu.VMEM((1, GRID), jnp.int32),
            pltpu.VMEM((1, GRID), jnp.int32),
            pltpu.VMEM((CHUNKS, GRID * CHUNK, LON_PAD), bf16),
            pltpu.VMEM((LAT_PAD, LAT_PAD), bf16),
            pltpu.VMEM((CHUNKS, GRID // 2, 2, BLOCK, LANES), bf16),
            pltpu.VMEM((CHUNKS, GRID, BLOCK, LANES), bf16),
            pltpu.VMEM((GRID * BLOCK, LANES), jnp.float32),
            pltpu.VMEM((CHUNKS, MEM // 2, 2, rows, LAT_PAD), bf16),
            pltpu.VMEM((CHUNKS, MEM, rows, LAT_PAD), bf16),
            dma((5,)), dma((CHUNKS,)), dma((CHUNKS,)), dma((CHUNKS,)), dma((CHUNKS,)), dma((CHUNKS,)), dma((CHUNKS,)),
        ],
        compiler_params=pltpu.CompilerParams(collective_id=0, has_side_effects=True, vmem_limit_bytes=60 * 1024 * 1024),
    )(jnp.transpose(control, (0, 2, 1, 3)), jnp.transpose(perturbation, (0, 2, 1, 3)), vertical,
      lat_counts.reshape(1, GRID), lon_counts.reshape(1, GRID))
    return jnp.transpose(summed.reshape(COLS, SHARE, LAT_PAD), (1, 0, 2))


def solution(mesh):
    in_specs = (P("mem", None, "grid", None), P("mem", None, "grid", None), P(), P(), P())
    out_specs = P("mem", "grid", None)
    return jax.shard_map(
        per_device, mesh=mesh, in_specs=in_specs, out_specs=out_specs, check_vma=False
    )
```

```python
import math

import jax
import jax.numpy as jnp
import numpy as np
from jax import lax
from jax.experimental import pallas as pl
from jax.experimental.pallas import tpu as pltpu
from jax.sharding import PartitionSpec as P

LAT = 361
LON = 720
LENGTH = 8
BAND = 48
MESH = pl.DeviceIdType.MESH
FAR = 20000.0
NORM = np.sqrt(np.sum(np.exp(np.float32(-2.0) * np.arange(BAND + 1, dtype=np.float32) / np.float32(LENGTH)), dtype=np.float32))
SCALE = float(np.float32(1.0) / NORM)

GRID = 64
SIDE = 8
MEM = 8
MEMBERS = 4
LEV = 32
ROWS = 6
COLS = 12
LON_PAD = GRID * COLS
LAT_PAD = GRID * ROWS
LANES = MEMBERS * LEV
CHUNK = 4
CHUNKS = COLS // CHUNK
PAIRS = ROWS // 2
BLOCK = CHUNK * ROWS
SHARE = LEV // MEM
TILE = 8
PIECES = ((0, 0, 1), (0, 1, 2), (1, 0, 3), (2, 0, 3))


def nt(a, b):
    return lax.dot_general(a, b, (((1,), (1,)), ((), ())), preferred_element_type=jnp.float32)


def iota(shape, dim):
    return lax.broadcasted_iota(jnp.int32, shape, dim)


def positions_down(counts, slab, place, missing):
    rows = slab.shape[0]
    devices = iota((rows, GRID), 1)
    table = jnp.broadcast_to(counts, (128, GRID)).astype(jnp.bfloat16)
    start = nt((devices < slab).astype(jnp.float32).astype(jnp.bfloat16), table)
    count = nt((devices == slab).astype(jnp.float32).astype(jnp.bfloat16), table)
    place = place.astype(jnp.float32)
    return jnp.where(place < count, start + place, missing)


def positions_across(counts, slab, place, missing):
    lanes = slab.shape[1]
    devices = iota((GRID, lanes), 0)
    table = jnp.broadcast_to(counts, (8, GRID)).astype(jnp.bfloat16)
    before = (devices < slab).astype(jnp.float32).astype(jnp.bfloat16)
    own = (devices == slab).astype(jnp.float32).astype(jnp.bfloat16)
    start = jnp.dot(table, before, preferred_element_type=jnp.float32)
    count = jnp.dot(table, own, preferred_element_type=jnp.float32)
    place = place.astype(jnp.float32)
    return jnp.where(place < count, start + place, missing)


def weights(lag, inside):
    return jnp.where(inside, jnp.exp(lag * (-1.0 / LENGTH)) * SCALE, 0.0).astype(jnp.bfloat16)


def interleave(first, second):
    low = iota(first.shape, 1) < 4
    even = jnp.where(low, first, pltpu.roll(second, 4, 1))
    odd = jnp.where(low, pltpu.roll(first, 4, 1), second)
    return even, odd


def kernel(control, perturbation, vertical, lat_counts, lon_counts, out,
           ctrl, pert, vert, latc, lonc, lon_t, lat_k, send, middle, recv, wide, part, parts,
           in_sem, mid_send_sem, mid_recv_sem, send_sem, recv_sem, own_sem, near_sem, psend_sem, precv_sem, pown_sem):
    me = lax.axis_index("grid")
    mine = lax.axis_index("mem")
    my_y, my_x, my_z = me // SIDE, (me % SIDE) // 2, me % 2

    def across(step):
        to_x, to_z = (my_x + step // 2) % 4, (my_z + step % 2) % 2
        return my_y * SIDE + to_x * 2 + to_z, to_x, to_z

    def along(step):
        to_y = (my_y + step) % SIDE
        return to_y * SIDE + me % SIDE, to_y

    loads = [pltpu.make_async_copy(source, target, in_sem.at[index]) for index, (source, target) in enumerate(
        ((lon_counts, lonc), (control, ctrl), (lat_counts, latc), (vertical, vert), (perturbation, pert)))]
    for load in loads:
        load.start()

    barrier = pltpu.get_barrier_semaphore()

    def greet(step, carry):
        pl.semaphore_signal(barrier, inc=1, device_id={"grid": across(step)[0]}, device_id_type=MESH)
        pl.semaphore_signal(barrier, inc=1, device_id={"grid": along(step)[0]}, device_id_type=MESH)
        pl.semaphore_signal(barrier, inc=1, device_id={"mem": (mine + step) % MEM}, device_id_type=MESH)
        return carry

    lax.fori_loop(1, SIDE, greet, 0)

    loads[0].wait()
    counts = lonc[...].astype(jnp.float32)
    lanes = iota((GRID, LON_PAD), 1)
    source = positions_across(counts, lanes // COLS, lanes[:8] % COLS, -FAR)
    for q in range(CHUNKS):
        rows = iota((GRID * CHUNK, GRID), 0)
        place = iota((GRID * CHUNK, 128), 0) % CHUNK + q * CHUNK
        target = positions_down(counts, rows // CHUNK, place, FAR)
        for tile in range(LON_PAD // 128):
            lag = target - source[:1, tile * 128:(tile + 1) * 128]
            lag = jnp.where(lag < 0, lag + LON, lag)
            lon_t[q, :, tile * 128:(tile + 1) * 128] = weights(lag, lag <= BAND)
        if q == 0:
            loads[1].wait()
        fields = jnp.concatenate([ctrl[:, i].reshape(LANES, LON_PAD) for i in range(ROWS)], axis=0)
        smooth = nt(lon_t[q], fields)
        for pair in range(PAIRS):
            first, second = [smooth[:, (2 * pair + half) * LANES:(2 * pair + half + 1) * LANES].reshape(GRID * CHUNK // 8, 8, LANES)
                             for half in range(2)]
            for parity, block in enumerate(interleave(first, second)):
                send[q, :, :, parity, pair * TILE:(pair + 1) * TILE, :] = block.astype(jnp.bfloat16).reshape(SIDE, 4, TILE, LANES)
        if q == 0:
            pl.semaphore_wait(barrier, 3 * (SIDE - 1))

        def direct(step, carry):
            peer, to_y = along(step)
            pltpu.make_async_remote_copy(
                src_ref=send.at[q, to_y, my_x, my_z], dst_ref=recv.at[q, my_y, 0],
                send_sem=send_sem.at[q], recv_sem=recv_sem.at[q],
                device_id={"grid": peer}, device_id_type=MESH).start()
            return carry

        lax.fori_loop(1, SIDE, direct, 0)
        for piece, (chunk, group, groups) in enumerate(PIECES):
            if chunk != q:
                continue
            span = pl.ds(group * TILE, groups * TILE)

            def spread(step, carry):
                peer, to_x, to_z = across(step)
                pltpu.make_async_remote_copy(
                    src_ref=send.at[q, :, to_x, to_z, span], dst_ref=middle.at[q, step - 1, :, span],
                    send_sem=mid_send_sem.at[piece], recv_sem=mid_recv_sem.at[piece],
                    device_id={"grid": peer}, device_id_type=MESH).start()
                return carry

            lax.fori_loop(1, SIDE, spread, 0)
        pltpu.make_async_copy(send.at[q, my_y, my_x, my_z], recv.at[q, my_y, 0], own_sem.at[q]).start()

    def pass_on(piece):
        q, group, groups = PIECES[piece]
        span = pl.ds(group * TILE, groups * TILE)
        pltpu.make_async_copy(middle.at[q, :, :, span], middle.at[q, :, :, span], mid_recv_sem.at[piece]).wait()

        def forward(step, carry):
            peer, to_y = along(step)
            pltpu.make_async_remote_copy(
                src_ref=middle.at[q, :, to_y, span], dst_ref=recv.at[q, my_y, pl.ds(1, SIDE - 1), span],
                send_sem=send_sem.at[q], recv_sem=recv_sem.at[q],
                device_id={"grid": peer}, device_id_type=MESH).start()
            return carry

        lax.fori_loop(1, SIDE, forward, 0)
        pltpu.make_async_copy(middle.at[q, :, my_y, span], recv.at[q, my_y, pl.ds(1, SIDE - 1), span], near_sem.at[piece]).start()

    pass_on(0)

    loads[2].wait()
    counts = latc[...].astype(jnp.float32)
    half_rows = GRID * PAIRS
    lanes = iota((GRID, LAT_PAD), 1)
    target = positions_across(counts, lanes // ROWS, lanes[:8] % ROWS, -FAR)
    block = iota((LAT_PAD, GRID), 0) % half_rows // PAIRS
    step = block % SIDE
    slab = block // SIDE * SIDE + (my_x + 4 - step // 2) % 4 * 2 + (my_z + 2 - step % 2) % 2
    long_rows = iota((LAT_PAD, 128), 0)
    place = 2 * (long_rows % PAIRS) + long_rows // half_rows
    source = positions_down(counts, slab, place, FAR)
    for tile in range(LAT_PAD // 128):
        lag = target[:1, tile * 128:(tile + 1) * 128] - source
        lat_k[:, tile * 128:(tile + 1) * 128] = weights(lag, (lag >= 0) & (lag <= BAND))

    loads[3].wait()
    spread_lanes = (iota((LEV, LANES), 0) == iota((LEV, LANES), 1) % LEV).astype(jnp.float32).astype(jnp.bfloat16)
    wide_factor = jnp.dot(vert[...], spread_lanes, preferred_element_type=jnp.float32)
    wide_factor = jnp.concatenate([wide_factor] * MEMBERS, axis=0)
    mixing = jnp.where(iota((LANES, LANES), 0) // LEV == iota((LANES, LANES), 1) // LEV, wide_factor, 0.0).astype(jnp.bfloat16)

    for piece in range(1, len(PIECES)):
        pass_on(piece)

    loads[4].wait()
    for q in range(CHUNKS):
        pltpu.make_async_copy(send.at[q, my_y, my_x, my_z], recv.at[q, my_y, 0], own_sem.at[q]).wait()
        for piece, (chunk, group, groups) in enumerate(PIECES):
            if chunk == q:
                span = pl.ds(group * TILE, groups * TILE)
                pltpu.make_async_copy(middle.at[q, :, my_y, span], recv.at[q, my_y, pl.ds(1, SIDE - 1), span], near_sem.at[piece]).wait()
        pltpu.make_async_copy(recv.at[q, pl.ds(0, SIDE - 1)], recv.at[q, pl.ds(0, SIDE - 1)], recv_sem.at[q]).wait()
        wide[...] = recv[q].astype(jnp.float32).reshape(GRID * BLOCK, LANES)
        mixed = []
        for c in range(CHUNK):
            fields = jnp.concatenate([wide[pl.ds(half * CHUNK + c, half_rows, stride=2 * CHUNK), :] for half in range(2)], axis=0)
            mixed.append(nt(mixing, fields.astype(jnp.bfloat16)).astype(jnp.bfloat16))
        filtered = jnp.dot(jnp.concatenate(mixed, axis=0), lat_k[...], preferred_element_type=jnp.float32)
        sums = []
        for c in range(CHUNK):
            field = filtered[c * LANES:(c + 1) * LANES].reshape(MEMBERS, LEV, LAT_PAD)
            sums.append(jnp.sum(field * pert[:, q * CHUNK + c].astype(jnp.float32), axis=0).reshape(LEV // 8, 8, LAT_PAD))
        for two in range(CHUNK // 2):
            for parity, block in enumerate(interleave(sums[2 * two], sums[2 * two + 1])):
                part[q, :, parity, two * TILE:(two + 1) * TILE, :] = block.astype(jnp.bfloat16)
        for step in range(1, MEM):
            peer = (mine + step) % MEM
            pltpu.make_async_remote_copy(
                src_ref=part.at[q, peer // 2, peer % 2], dst_ref=parts.at[q, mine],
                send_sem=psend_sem.at[q], recv_sem=precv_sem.at[q],
                device_id={"mem": peer}, device_id_type=MESH).start()
        pltpu.make_async_copy(part.at[q, mine // 2, mine % 2], parts.at[q, mine], pown_sem.at[q]).start()

    rows = CHUNK * SHARE
    for q in range(CHUNKS):
        pltpu.make_async_copy(part.at[q, mine // 2, mine % 2], parts.at[q, mine], pown_sem.at[q]).wait()
        pltpu.make_async_copy(parts.at[q, pl.ds(0, MEM - 1)], parts.at[q, pl.ds(0, MEM - 1)], precv_sem.at[q]).wait()
        out[q * rows:(q + 1) * rows, :] = jnp.sum(parts[q].astype(jnp.float32), axis=0)
    for piece, (q, group, groups) in enumerate(PIECES):
        span = pl.ds(group * TILE, groups * TILE)
        pltpu.make_async_copy(middle.at[q, :, :, span], middle.at[q, :, :, span], mid_send_sem.at[piece]).wait()
    for q in range(CHUNKS):
        pltpu.make_async_copy(recv.at[q, pl.ds(0, SIDE - 1)], recv.at[q, pl.ds(0, SIDE - 1)], send_sem.at[q]).wait()
        pltpu.make_async_copy(parts.at[q, pl.ds(0, MEM - 1)], parts.at[q, pl.ds(0, MEM - 1)], psend_sem.at[q]).wait()


def per_device(control, perturbation, vertical, lat_counts, lon_counts):
    bf16 = jnp.bfloat16
    dma = pltpu.SemaphoreType.DMA
    rows = CHUNK * SHARE
    summed = pl.pallas_call(
        kernel,
        out_shape=jax.ShapeDtypeStruct((COLS * SHARE, LAT_PAD), jnp.float32),
        in_specs=[pl.BlockSpec(memory_space=pltpu.HBM)] * 5,
        out_specs=pl.BlockSpec(memory_space=pltpu.VMEM),
        scratch_shapes=[
            pltpu.VMEM((MEMBERS, ROWS, LEV, LON_PAD), bf16),
            pltpu.VMEM((MEMBERS, COLS, LEV, LAT_PAD), bf16),
            pltpu.VMEM((LEV, LEV), bf16),
            pltpu.VMEM((1, GRID), jnp.int32),
            pltpu.VMEM((1, GRID), jnp.int32),
            pltpu.VMEM((CHUNKS, GRID * CHUNK, LON_PAD), bf16),
            pltpu.VMEM((LAT_PAD, LAT_PAD), bf16),
            pltpu.VMEM((CHUNKS, SIDE, 4, 2, BLOCK, LANES), bf16),
            pltpu.VMEM((CHUNKS, SIDE - 1, SIDE, BLOCK, LANES), bf16),
            pltpu.VMEM((CHUNKS, SIDE, SIDE, BLOCK, LANES), bf16),
            pltpu.VMEM((GRID * BLOCK, LANES), jnp.float32),
            pltpu.VMEM((CHUNKS, MEM // 2, 2, rows, LAT_PAD), bf16),
            pltpu.VMEM((CHUNKS, MEM, rows, LAT_PAD), bf16),
            dma((5,)), dma((len(PIECES),)), dma((len(PIECES),)), dma((CHUNKS,)), dma((CHUNKS,)), dma((CHUNKS,)),
            dma((len(PIECES),)), dma((CHUNKS,)), dma((CHUNKS,)), dma((CHUNKS,)),
        ],
        compiler_params=pltpu.CompilerParams(collective_id=0, has_side_effects=True, vmem_limit_bytes=60 * 1024 * 1024),
    )(jnp.transpose(control, (0, 2, 1, 3)), jnp.transpose(perturbation, (0, 2, 1, 3)), vertical,
      lat_counts.reshape(1, GRID), lon_counts.reshape(1, GRID))
    return jnp.transpose(summed.reshape(COLS, SHARE, LAT_PAD), (1, 0, 2))


def solution(mesh):
    in_specs = (P("mem", None, "grid", None), P("mem", None, "grid", None), P(), P(), P())
    out_specs = P("mem", "grid", None)
    return jax.shard_map(
        per_device, mesh=mesh, in_specs=in_specs, out_specs=out_specs, check_vma=False
    )
```

```python
import math

import jax
import jax.numpy as jnp
import numpy as np
from jax import lax
from jax.experimental import pallas as pl
from jax.experimental.pallas import tpu as pltpu
from jax.sharding import PartitionSpec as P

LAT = 361
LON = 720
LENGTH = 8
BAND = 48
MESH = pl.DeviceIdType.MESH
FAR = 20000.0
NORM = np.sqrt(np.sum(np.exp(np.float32(-2.0) * np.arange(BAND + 1, dtype=np.float32) / np.float32(LENGTH)), dtype=np.float32))
SCALE = float(np.float32(1.0) / NORM)

GRID = 64
SIDE = 8
MEM = 8
MEMBERS = 4
LEV = 32
ROWS = 6
COLS = 12
LON_PAD = GRID * COLS
LAT_PAD = GRID * ROWS
LANES = MEMBERS * LEV
CHUNK = 4
CHUNKS = COLS // CHUNK
PAIRS = ROWS // 2
BLOCK = CHUNK * ROWS
SHARE = LEV // MEM
TILE = 8
PIECES = ((0, 0, 1), (0, 1, 2), (1, 0, 3), (2, 0, 3))


def nt(a, b):
    return lax.dot_general(a, b, (((1,), (1,)), ((), ())), preferred_element_type=jnp.float32)


def iota(shape, dim):
    return lax.broadcasted_iota(jnp.int32, shape, dim)


def positions_down(counts, slab, place, missing):
    rows = slab.shape[0]
    devices = iota((rows, GRID), 1)
    table = jnp.broadcast_to(counts, (128, GRID)).astype(jnp.bfloat16)
    start = nt((devices < slab).astype(jnp.float32).astype(jnp.bfloat16), table)
    count = nt((devices == slab).astype(jnp.float32).astype(jnp.bfloat16), table)
    place = place.astype(jnp.float32)
    return jnp.where(place < count, start + place, missing)


def positions_across(counts, slab, place, missing):
    lanes = slab.shape[1]
    devices = iota((GRID, lanes), 0)
    table = jnp.broadcast_to(counts, (8, GRID)).astype(jnp.bfloat16)
    before = (devices < slab).astype(jnp.float32).astype(jnp.bfloat16)
    own = (devices == slab).astype(jnp.float32).astype(jnp.bfloat16)
    start = jnp.dot(table, before, preferred_element_type=jnp.float32)
    count = jnp.dot(table, own, preferred_element_type=jnp.float32)
    place = place.astype(jnp.float32)
    return jnp.where(place < count, start + place, missing)


def weights(lag, inside):
    return jnp.where(inside, jnp.exp(lag * (-1.0 / LENGTH)) * SCALE, 0.0).astype(jnp.bfloat16)


def interleave(first, second):
    low = iota(first.shape, 1) < 4
    even = jnp.where(low, first, pltpu.roll(second, 4, 1))
    odd = jnp.where(low, pltpu.roll(first, 4, 1), second)
    return even, odd


def kernel(control, perturbation, vertical, lat_counts, lon_counts, out,
           ctrl, pert, vert, latc, lonc, lon_t, lat_k, send, middle, recv, wide, part, parts,
           in_sem, mid_send_sem, mid_recv_sem, send_sem, recv_sem, own_sem, near_sem, psend_sem, precv_sem, pown_sem):
    me = lax.axis_index("grid")
    mine = lax.axis_index("mem")
    my_y, my_x, my_z = me // SIDE, (me % SIDE) // 2, me % 2

    def across(step):
        to_x, to_z = (my_x + step // 2) % 4, (my_z + step % 2) % 2
        return my_y * SIDE + to_x * 2 + to_z, to_x, to_z

    def along(step):
        to_y = (my_y + 4 + (step // 2) * (2 * (step % 2) - 1)) % SIDE
        return to_y * SIDE + me % SIDE, to_y

    barrier = pltpu.get_barrier_semaphore()

    def greet(step, carry):
        pl.semaphore_signal(barrier, inc=1, device_id={"grid": across(step)[0]}, device_id_type=MESH)
        pl.semaphore_signal(barrier, inc=1, device_id={"grid": along(step)[0]}, device_id_type=MESH)
        pl.semaphore_signal(barrier, inc=1, device_id={"mem": (mine + step) % MEM}, device_id_type=MESH)
        return carry

    lax.fori_loop(1, SIDE, greet, 0)

    loads = [pltpu.make_async_copy(source, target, in_sem.at[index]) for index, (source, target) in enumerate(
        ((lon_counts, lonc), (control, ctrl), (lat_counts, latc), (vertical, vert), (perturbation, pert)))]
    for load in loads:
        load.start()

    loads[0].wait()
    counts = lonc[...].astype(jnp.float32)
    lanes = iota((GRID, LON_PAD), 1)
    source = positions_across(counts, lanes // COLS, lanes[:8] % COLS, -FAR)
    def smooth_chunk(q):
        rows = iota((GRID * CHUNK, GRID), 0)
        place = iota((GRID * CHUNK, 128), 0) % CHUNK + q * CHUNK
        target = positions_down(counts, rows // CHUNK, place, FAR)
        for tile in range(LON_PAD // 128):
            lag = target - source[:1, tile * 128:(tile + 1) * 128]
            lag = jnp.where(lag < 0, lag + LON, lag)
            lon_t[q, :, tile * 128:(tile + 1) * 128] = weights(lag, lag <= BAND)
        if q == 0:
            loads[1].wait()
        fields = jnp.concatenate([ctrl[:, i].reshape(LANES, LON_PAD) for i in range(ROWS)], axis=0)
        smooth = nt(lon_t[q], fields)
        for pair in range(PAIRS):
            first, second = [smooth[:, (2 * pair + half) * LANES:(2 * pair + half + 1) * LANES].reshape(GRID * CHUNK // 8, 8, LANES)
                             for half in range(2)]
            for parity, block in enumerate(interleave(first, second)):
                send[q, :, :, parity, pair * TILE:(pair + 1) * TILE, :] = block.astype(jnp.bfloat16).reshape(SIDE, 4, TILE, LANES)

    def send_direct(q):
        def direct(step, carry):
            peer, to_y = along(step)
            pltpu.make_async_remote_copy(
                src_ref=send.at[q, to_y, my_x, my_z], dst_ref=recv.at[q, my_y, 0],
                send_sem=send_sem.at[q], recv_sem=recv_sem.at[q],
                device_id={"grid": peer}, device_id_type=MESH).start()
            return carry

        lax.fori_loop(1, SIDE, direct, 0)

    def send_piece(piece):
        q, group, groups = PIECES[piece]
        span = pl.ds(group * TILE, groups * TILE)

        def spread(step, carry):
            peer, to_x, to_z = across(step)
            pltpu.make_async_remote_copy(
                src_ref=send.at[q, :, to_x, to_z, span], dst_ref=middle.at[q, step - 1, :, span],
                send_sem=mid_send_sem.at[piece], recv_sem=mid_recv_sem.at[piece],
                device_id={"grid": peer}, device_id_type=MESH).start()
            return carry

        lax.fori_loop(1, SIDE, spread, 0)

    def keep(q):
        pltpu.make_async_copy(send.at[q, my_y, my_x, my_z], recv.at[q, my_y, 0], own_sem.at[q]).start()

    def pass_on(piece):
        q, group, groups = PIECES[piece]
        span = pl.ds(group * TILE, groups * TILE)
        pltpu.make_async_copy(middle.at[q, :, :, span], middle.at[q, :, :, span], mid_recv_sem.at[piece]).wait()

        def forward(step, carry):
            peer, to_y = along(step)
            pltpu.make_async_remote_copy(
                src_ref=middle.at[q, :, to_y, span], dst_ref=recv.at[q, my_y, pl.ds(1, SIDE - 1), span],
                send_sem=send_sem.at[q], recv_sem=recv_sem.at[q],
                device_id={"grid": peer}, device_id_type=MESH).start()
            return carry

        lax.fori_loop(1, SIDE, forward, 0)
        pltpu.make_async_copy(middle.at[q, :, my_y, span], recv.at[q, my_y, pl.ds(1, SIDE - 1), span], near_sem.at[piece]).start()

    smooth_chunk(0)
    pl.semaphore_wait(barrier, 3 * (SIDE - 1))
    send_piece(0)
    send_direct(0)
    send_piece(1)
    smooth_chunk(1)
    send_direct(1)
    send_piece(2)
    smooth_chunk(2)
    pass_on(0)
    send_direct(2)
    send_piece(3)
    for q in range(CHUNKS):
        keep(q)
    pass_on(1)

    loads[2].wait()
    counts = latc[...].astype(jnp.float32)
    half_rows = GRID * PAIRS
    lanes = iota((GRID, LAT_PAD), 1)
    target = positions_across(counts, lanes // ROWS, lanes[:8] % ROWS, -FAR)
    block = iota((LAT_PAD, GRID), 0) % half_rows // PAIRS
    step = block % SIDE
    slab = block // SIDE * SIDE + (my_x + 4 - step // 2) % 4 * 2 + (my_z + 2 - step % 2) % 2
    long_rows = iota((LAT_PAD, 128), 0)
    place = 2 * (long_rows % PAIRS) + long_rows // half_rows
    source = positions_down(counts, slab, place, FAR)
    for tile in range(LAT_PAD // 128):
        lag = target[:1, tile * 128:(tile + 1) * 128] - source
        lat_k[:, tile * 128:(tile + 1) * 128] = weights(lag, (lag >= 0) & (lag <= BAND))

    loads[3].wait()
    spread_lanes = (iota((LEV, LANES), 0) == iota((LEV, LANES), 1) % LEV).astype(jnp.float32).astype(jnp.bfloat16)
    wide_factor = jnp.dot(vert[...], spread_lanes, preferred_element_type=jnp.float32)
    wide_factor = jnp.concatenate([wide_factor] * MEMBERS, axis=0)
    mixing = jnp.where(iota((LANES, LANES), 0) // LEV == iota((LANES, LANES), 1) // LEV, wide_factor, 0.0).astype(jnp.bfloat16)

    for piece in range(2, len(PIECES)):
        pass_on(piece)

    loads[4].wait()
    for q in range(CHUNKS):
        pltpu.make_async_copy(send.at[q, my_y, my_x, my_z], recv.at[q, my_y, 0], own_sem.at[q]).wait()
        for piece, (chunk, group, groups) in enumerate(PIECES):
            if chunk == q:
                span = pl.ds(group * TILE, groups * TILE)
                pltpu.make_async_copy(middle.at[q, :, my_y, span], recv.at[q, my_y, pl.ds(1, SIDE - 1), span], near_sem.at[piece]).wait()
        pltpu.make_async_copy(recv.at[q, pl.ds(0, SIDE - 1)], recv.at[q, pl.ds(0, SIDE - 1)], recv_sem.at[q]).wait()
        wide[...] = recv[q].astype(jnp.float32).reshape(GRID * BLOCK, LANES)
        mixed = []
        for c in range(CHUNK):
            fields = jnp.concatenate([wide[pl.ds(half * CHUNK + c, half_rows, stride=2 * CHUNK), :] for half in range(2)], axis=0)
            mixed.append(nt(mixing, fields.astype(jnp.bfloat16)).astype(jnp.bfloat16))
        filtered = jnp.dot(jnp.concatenate(mixed, axis=0), lat_k[...], preferred_element_type=jnp.float32)
        sums = []
        for c in range(CHUNK):
            field = filtered[c * LANES:(c + 1) * LANES].reshape(MEMBERS, LEV, LAT_PAD)
            sums.append(jnp.sum(field * pert[:, q * CHUNK + c].astype(jnp.float32), axis=0).reshape(LEV // 8, 8, LAT_PAD))
        for two in range(CHUNK // 2):
            for parity, block in enumerate(interleave(sums[2 * two], sums[2 * two + 1])):
                part[q, :, parity, two * TILE:(two + 1) * TILE, :] = block.astype(jnp.bfloat16)
        for step in range(1, MEM):
            peer = (mine + step) % MEM
            pltpu.make_async_remote_copy(
                src_ref=part.at[q, peer // 2, peer % 2], dst_ref=parts.at[q, mine],
                send_sem=psend_sem.at[q], recv_sem=precv_sem.at[q],
                device_id={"mem": peer}, device_id_type=MESH).start()
        pltpu.make_async_copy(part.at[q, mine // 2, mine % 2], parts.at[q, mine], pown_sem.at[q]).start()

    rows = CHUNK * SHARE
    for q in range(CHUNKS):
        pltpu.make_async_copy(part.at[q, mine // 2, mine % 2], parts.at[q, mine], pown_sem.at[q]).wait()
        pltpu.make_async_copy(parts.at[q, pl.ds(0, MEM - 1)], parts.at[q, pl.ds(0, MEM - 1)], precv_sem.at[q]).wait()
        out[q * rows:(q + 1) * rows, :] = jnp.sum(parts[q].astype(jnp.float32), axis=0)
    for piece, (q, group, groups) in enumerate(PIECES):
        span = pl.ds(group * TILE, groups * TILE)
        pltpu.make_async_copy(middle.at[q, :, :, span], middle.at[q, :, :, span], mid_send_sem.at[piece]).wait()
    for q in range(CHUNKS):
        pltpu.make_async_copy(recv.at[q, pl.ds(0, SIDE - 1)], recv.at[q, pl.ds(0, SIDE - 1)], send_sem.at[q]).wait()
        pltpu.make_async_copy(parts.at[q, pl.ds(0, MEM - 1)], parts.at[q, pl.ds(0, MEM - 1)], psend_sem.at[q]).wait()


def per_device(control, perturbation, vertical, lat_counts, lon_counts):
    bf16 = jnp.bfloat16
    dma = pltpu.SemaphoreType.DMA
    rows = CHUNK * SHARE
    summed = pl.pallas_call(
        kernel,
        out_shape=jax.ShapeDtypeStruct((COLS * SHARE, LAT_PAD), jnp.float32),
        in_specs=[pl.BlockSpec(memory_space=pltpu.HBM)] * 5,
        out_specs=pl.BlockSpec(memory_space=pltpu.VMEM),
        scratch_shapes=[
            pltpu.VMEM((MEMBERS, ROWS, LEV, LON_PAD), bf16),
            pltpu.VMEM((MEMBERS, COLS, LEV, LAT_PAD), bf16),
            pltpu.VMEM((LEV, LEV), bf16),
            pltpu.VMEM((1, GRID), jnp.int32),
            pltpu.VMEM((1, GRID), jnp.int32),
            pltpu.VMEM((CHUNKS, GRID * CHUNK, LON_PAD), bf16),
            pltpu.VMEM((LAT_PAD, LAT_PAD), bf16),
            pltpu.VMEM((CHUNKS, SIDE, 4, 2, BLOCK, LANES), bf16),
            pltpu.VMEM((CHUNKS, SIDE - 1, SIDE, BLOCK, LANES), bf16),
            pltpu.VMEM((CHUNKS, SIDE, SIDE, BLOCK, LANES), bf16),
            pltpu.VMEM((GRID * BLOCK, LANES), jnp.float32),
            pltpu.VMEM((CHUNKS, MEM // 2, 2, rows, LAT_PAD), bf16),
            pltpu.VMEM((CHUNKS, MEM, rows, LAT_PAD), bf16),
            dma((5,)), dma((len(PIECES),)), dma((len(PIECES),)), dma((CHUNKS,)), dma((CHUNKS,)), dma((CHUNKS,)),
            dma((len(PIECES),)), dma((CHUNKS,)), dma((CHUNKS,)), dma((CHUNKS,)),
        ],
        compiler_params=pltpu.CompilerParams(collective_id=0, has_side_effects=True, vmem_limit_bytes=60 * 1024 * 1024),
    )(jnp.transpose(control, (0, 2, 1, 3)), jnp.transpose(perturbation, (0, 2, 1, 3)), vertical,
      lat_counts.reshape(1, GRID), lon_counts.reshape(1, GRID))
    return jnp.transpose(summed.reshape(COLS, SHARE, LAT_PAD), (1, 0, 2))


def solution(mesh):
    in_specs = (P("mem", None, "grid", None), P("mem", None, "grid", None), P(), P(), P())
    out_specs = P("mem", "grid", None)
    return jax.shard_map(
        per_device, mesh=mesh, in_specs=in_specs, out_specs=out_specs, check_vma=False
    )
```

```python
import math

import jax
import jax.numpy as jnp
import numpy as np
from jax import lax
from jax.experimental import pallas as pl
from jax.experimental.pallas import tpu as pltpu
from jax.sharding import PartitionSpec as P

LAT = 361
LON = 720
LENGTH = 8
BAND = 48
MESH = pl.DeviceIdType.MESH
FAR = 20000.0
NORM = np.sqrt(np.sum(np.exp(np.float32(-2.0) * np.arange(BAND + 1, dtype=np.float32) / np.float32(LENGTH)), dtype=np.float32))
SCALE = float(np.float32(1.0) / NORM)

GRID = 64
SIDE = 8
MEM = 8
MEMBERS = 4
LEV = 32
ROWS = 6
COLS = 12
LON_PAD = GRID * COLS
LAT_PAD = GRID * ROWS
LANES = MEMBERS * LEV
CHUNK = 4
CHUNKS = COLS // CHUNK
PAIRS = ROWS // 2
BLOCK = CHUNK * ROWS
SHARE = LEV // MEM
TILE = 8
PIECES = ((1, 0, 3), (2, 0, 3))


def nt(a, b):
    return lax.dot_general(a, b, (((1,), (1,)), ((), ())), preferred_element_type=jnp.float32)


def iota(shape, dim):
    return lax.broadcasted_iota(jnp.int32, shape, dim)


def positions_down(counts, slab, place, missing):
    rows = slab.shape[0]
    devices = iota((rows, GRID), 1)
    table = jnp.broadcast_to(counts, (128, GRID)).astype(jnp.bfloat16)
    start = nt((devices < slab).astype(jnp.float32).astype(jnp.bfloat16), table)
    count = nt((devices == slab).astype(jnp.float32).astype(jnp.bfloat16), table)
    place = place.astype(jnp.float32)
    return jnp.where(place < count, start + place, missing)


def positions_across(counts, slab, place, missing):
    lanes = slab.shape[1]
    devices = iota((GRID, lanes), 0)
    table = jnp.broadcast_to(counts, (8, GRID)).astype(jnp.bfloat16)
    before = (devices < slab).astype(jnp.float32).astype(jnp.bfloat16)
    own = (devices == slab).astype(jnp.float32).astype(jnp.bfloat16)
    start = jnp.dot(table, before, preferred_element_type=jnp.float32)
    count = jnp.dot(table, own, preferred_element_type=jnp.float32)
    place = place.astype(jnp.float32)
    return jnp.where(place < count, start + place, missing)


def weights(lag, inside):
    return jnp.where(inside, jnp.exp(lag * (-1.0 / LENGTH)) * SCALE, 0.0).astype(jnp.bfloat16)


def interleave(first, second):
    low = iota(first.shape, 1) < 4
    even = jnp.where(low, first, pltpu.roll(second, 4, 1))
    odd = jnp.where(low, pltpu.roll(first, 4, 1), second)
    return even, odd


def kernel(control, perturbation, vertical, lat_counts, lon_counts, out,
           ctrl, pert, vert, latc, lonc, lon_t, lat_k, send, column, middle, recv, wide, part, parts,
           in_sem, mid_send_sem, mid_recv_sem, send_sem, recv_sem, own_sem, near_sem, psend_sem, precv_sem, pown_sem, col_send_sem, col_recv_sem, col_own_sem):
    me = lax.axis_index("grid")
    mine = lax.axis_index("mem")
    my_y, my_x, my_z = me // SIDE, (me % SIDE) // 2, me % 2

    def across(step):
        to_x, to_z = (my_x + step // 2) % 4, (my_z + step % 2) % 2
        return my_y * SIDE + to_x * 2 + to_z, to_x, to_z

    def along(step):
        to_y = (my_y + 4 + (step // 2) * (2 * (step % 2) - 1)) % SIDE
        return to_y * SIDE + me % SIDE, to_y

    barrier = pltpu.get_barrier_semaphore()

    def greet(step, carry):
        pl.semaphore_signal(barrier, inc=1, device_id={"grid": across(step)[0]}, device_id_type=MESH)
        pl.semaphore_signal(barrier, inc=1, device_id={"grid": along(step)[0]}, device_id_type=MESH)
        pl.semaphore_signal(barrier, inc=1, device_id={"mem": (mine + step) % MEM}, device_id_type=MESH)
        return carry

    lax.fori_loop(1, SIDE, greet, 0)

    loads = [pltpu.make_async_copy(source, target, in_sem.at[index]) for index, (source, target) in enumerate(
        ((lon_counts, lonc), (control, ctrl), (lat_counts, latc), (vertical, vert), (perturbation, pert)))]
    for load in loads:
        load.start()

    loads[0].wait()
    counts = lonc[...].astype(jnp.float32)
    lanes = iota((GRID, LON_PAD), 1)
    source = positions_across(counts, lanes // COLS, lanes[:8] % COLS, -FAR)
    def smooth_chunk(q):
        rows = iota((GRID * CHUNK, GRID), 0)
        place = iota((GRID * CHUNK, 128), 0) % CHUNK + q * CHUNK
        target = positions_down(counts, rows // CHUNK, place, FAR)
        for tile in range(LON_PAD // 128):
            lag = target - source[:1, tile * 128:(tile + 1) * 128]
            lag = jnp.where(lag < 0, lag + LON, lag)
            lon_t[q, :, tile * 128:(tile + 1) * 128] = weights(lag, lag <= BAND)
        if q == 0:
            loads[1].wait()
        fields = jnp.concatenate([ctrl[:, i].reshape(LANES, LON_PAD) for i in range(ROWS)], axis=0)
        smooth = nt(lon_t[q], fields)
        for pair in range(PAIRS):
            first, second = [smooth[:, (2 * pair + half) * LANES:(2 * pair + half + 1) * LANES].reshape(GRID * CHUNK // 8, 8, LANES)
                             for half in range(2)]
            for parity, block in enumerate(interleave(first, second)):
                send[q, :, :, parity, pair * TILE:(pair + 1) * TILE, :] = block.astype(jnp.bfloat16).reshape(SIDE, 4, TILE, LANES)

    def send_direct(q):
        def direct(step, carry):
            peer, to_y = along(step)
            pltpu.make_async_remote_copy(
                src_ref=send.at[q, to_y, my_x, my_z], dst_ref=recv.at[q, my_y, 0],
                send_sem=send_sem.at[q], recv_sem=recv_sem.at[q],
                device_id={"grid": peer}, device_id_type=MESH).start()
            return carry

        lax.fori_loop(1, SIDE, direct, 0)

    stay = pltpu.make_async_copy(send.at[0, my_y], column.at[my_y], own_sem.at[0])
    settle = pltpu.make_async_copy(column.at[:, my_x, my_z], recv.at[0, :, 0], col_own_sem.at[0])

    def send_column():
        def far(step, carry):
            peer, to_y = along(step)
            pltpu.make_async_remote_copy(
                src_ref=send.at[0, to_y], dst_ref=column.at[my_y],
                send_sem=col_send_sem.at[0], recv_sem=col_recv_sem.at[0],
                device_id={"grid": peer}, device_id_type=MESH).start()
            return carry

        lax.fori_loop(1, SIDE, far, 0)
        stay.start()

    def pass_column():
        stay.wait()
        pltpu.make_async_copy(column.at[pl.ds(0, SIDE - 1)], column.at[pl.ds(0, SIDE - 1)], col_recv_sem.at[0]).wait()

        def near(step, carry):
            peer, to_x, to_z = across(step)
            pltpu.make_async_remote_copy(
                src_ref=column.at[:, to_x, to_z], dst_ref=recv.at[0, :, step],
                send_sem=send_sem.at[0], recv_sem=recv_sem.at[0],
                device_id={"grid": peer}, device_id_type=MESH).start()
            return carry

        lax.fori_loop(1, SIDE, near, 0)
        settle.start()

    def send_piece(piece):
        q, group, groups = PIECES[piece]
        span = pl.ds(group * TILE, groups * TILE)

        def spread(step, carry):
            peer, to_x, to_z = across(step)
            pltpu.make_async_remote_copy(
                src_ref=send.at[q, :, to_x, to_z, span], dst_ref=middle.at[q, step - 1, :, span],
                send_sem=mid_send_sem.at[piece], recv_sem=mid_recv_sem.at[piece],
                device_id={"grid": peer}, device_id_type=MESH).start()
            return carry

        lax.fori_loop(1, SIDE, spread, 0)

    def keep(q):
        pltpu.make_async_copy(send.at[q, my_y, my_x, my_z], recv.at[q, my_y, 0], own_sem.at[q]).start()

    def pass_on(piece):
        q, group, groups = PIECES[piece]
        span = pl.ds(group * TILE, groups * TILE)
        pltpu.make_async_copy(middle.at[q, :, :, span], middle.at[q, :, :, span], mid_recv_sem.at[piece]).wait()

        def forward(step, carry):
            peer, to_y = along(step)
            pltpu.make_async_remote_copy(
                src_ref=middle.at[q, :, to_y, span], dst_ref=recv.at[q, my_y, pl.ds(1, SIDE - 1), span],
                send_sem=send_sem.at[q], recv_sem=recv_sem.at[q],
                device_id={"grid": peer}, device_id_type=MESH).start()
            return carry

        lax.fori_loop(1, SIDE, forward, 0)
        pltpu.make_async_copy(middle.at[q, :, my_y, span], recv.at[q, my_y, pl.ds(1, SIDE - 1), span], near_sem.at[piece]).start()

    smooth_chunk(0)
    pl.semaphore_wait(barrier, 3 * (SIDE - 1))
    send_column()
    smooth_chunk(1)
    send_piece(0)
    send_direct(1)
    smooth_chunk(2)
    send_piece(1)
    send_direct(2)
    for q in range(1, CHUNKS):
        keep(q)

    loads[2].wait()
    counts = latc[...].astype(jnp.float32)
    half_rows = GRID * PAIRS
    lanes = iota((GRID, LAT_PAD), 1)
    target = positions_across(counts, lanes // ROWS, lanes[:8] % ROWS, -FAR)
    block = iota((LAT_PAD, GRID), 0) % half_rows // PAIRS
    step = block % SIDE
    slab = block // SIDE * SIDE + (my_x + 4 - step // 2) % 4 * 2 + (my_z + 2 - step % 2) % 2
    long_rows = iota((LAT_PAD, 128), 0)
    place = 2 * (long_rows % PAIRS) + long_rows // half_rows
    source = positions_down(counts, slab, place, FAR)
    for tile in range(LAT_PAD // 128):
        lag = target[:1, tile * 128:(tile + 1) * 128] - source
        lat_k[:, tile * 128:(tile + 1) * 128] = weights(lag, (lag >= 0) & (lag <= BAND))

    loads[3].wait()
    spread_lanes = (iota((LEV, LANES), 0) == iota((LEV, LANES), 1) % LEV).astype(jnp.float32).astype(jnp.bfloat16)
    wide_factor = jnp.dot(vert[...], spread_lanes, preferred_element_type=jnp.float32)
    wide_factor = jnp.concatenate([wide_factor] * MEMBERS, axis=0)
    mixing = jnp.where(iota((LANES, LANES), 0) // LEV == iota((LANES, LANES), 1) // LEV, wide_factor, 0.0).astype(jnp.bfloat16)

    pass_on(0)
    pass_column()
    pass_on(1)

    loads[4].wait()
    for q in range(CHUNKS):
        if q == 0:
            settle.wait()
        else:
            pltpu.make_async_copy(send.at[q, my_y, my_x, my_z], recv.at[q, my_y, 0], own_sem.at[q]).wait()
        for piece, (chunk, group, groups) in enumerate(PIECES):
            if chunk == q:
                span = pl.ds(group * TILE, groups * TILE)
                pltpu.make_async_copy(middle.at[q, :, my_y, span], recv.at[q, my_y, pl.ds(1, SIDE - 1), span], near_sem.at[piece]).wait()
        pltpu.make_async_copy(recv.at[q, pl.ds(0, SIDE - 1)], recv.at[q, pl.ds(0, SIDE - 1)], recv_sem.at[q]).wait()
        wide[...] = recv[q].astype(jnp.float32).reshape(GRID * BLOCK, LANES)
        mixed = []
        for c in range(CHUNK):
            fields = jnp.concatenate([wide[pl.ds(half * CHUNK + c, half_rows, stride=2 * CHUNK), :] for half in range(2)], axis=0)
            mixed.append(nt(mixing, fields.astype(jnp.bfloat16)).astype(jnp.bfloat16))
        filtered = jnp.dot(jnp.concatenate(mixed, axis=0), lat_k[...], preferred_element_type=jnp.float32)
        sums = []
        for c in range(CHUNK):
            field = filtered[c * LANES:(c + 1) * LANES].reshape(MEMBERS, LEV, LAT_PAD)
            sums.append(jnp.sum(field * pert[:, q * CHUNK + c].astype(jnp.float32), axis=0).reshape(LEV // 8, 8, LAT_PAD))
        for two in range(CHUNK // 2):
            for parity, block in enumerate(interleave(sums[2 * two], sums[2 * two + 1])):
                part[q, :, parity, two * TILE:(two + 1) * TILE, :] = block.astype(jnp.bfloat16)
        for step in range(1, MEM):
            peer = (mine + step) % MEM
            pltpu.make_async_remote_copy(
                src_ref=part.at[q, peer // 2, peer % 2], dst_ref=parts.at[q, mine],
                send_sem=psend_sem.at[q], recv_sem=precv_sem.at[q],
                device_id={"mem": peer}, device_id_type=MESH).start()
        pltpu.make_async_copy(part.at[q, mine // 2, mine % 2], parts.at[q, mine], pown_sem.at[q]).start()

    rows = CHUNK * SHARE
    for q in range(CHUNKS):
        pltpu.make_async_copy(part.at[q, mine // 2, mine % 2], parts.at[q, mine], pown_sem.at[q]).wait()
        pltpu.make_async_copy(parts.at[q, pl.ds(0, MEM - 1)], parts.at[q, pl.ds(0, MEM - 1)], precv_sem.at[q]).wait()
        out[q * rows:(q + 1) * rows, :] = jnp.sum(parts[q].astype(jnp.float32), axis=0)
    pltpu.make_async_copy(column.at[pl.ds(0, SIDE - 1)], column.at[pl.ds(0, SIDE - 1)], col_send_sem.at[0]).wait()
    for piece, (q, group, groups) in enumerate(PIECES):
        span = pl.ds(group * TILE, groups * TILE)
        pltpu.make_async_copy(middle.at[q, :, :, span], middle.at[q, :, :, span], mid_send_sem.at[piece]).wait()
    for q in range(CHUNKS):
        pltpu.make_async_copy(recv.at[q, pl.ds(0, SIDE - 1)], recv.at[q, pl.ds(0, SIDE - 1)], send_sem.at[q]).wait()
        pltpu.make_async_copy(parts.at[q, pl.ds(0, MEM - 1)], parts.at[q, pl.ds(0, MEM - 1)], psend_sem.at[q]).wait()


def per_device(control, perturbation, vertical, lat_counts, lon_counts):
    bf16 = jnp.bfloat16
    dma = pltpu.SemaphoreType.DMA
    rows = CHUNK * SHARE
    summed = pl.pallas_call(
        kernel,
        out_shape=jax.ShapeDtypeStruct((COLS * SHARE, LAT_PAD), jnp.float32),
        in_specs=[pl.BlockSpec(memory_space=pltpu.HBM)] * 5,
        out_specs=pl.BlockSpec(memory_space=pltpu.VMEM),
        scratch_shapes=[
            pltpu.VMEM((MEMBERS, ROWS, LEV, LON_PAD), bf16),
            pltpu.VMEM((MEMBERS, COLS, LEV, LAT_PAD), bf16),
            pltpu.VMEM((LEV, LEV), bf16),
            pltpu.VMEM((1, GRID), jnp.int32),
            pltpu.VMEM((1, GRID), jnp.int32),
            pltpu.VMEM((CHUNKS, GRID * CHUNK, LON_PAD), bf16),
            pltpu.VMEM((LAT_PAD, LAT_PAD), bf16),
            pltpu.VMEM((CHUNKS, SIDE, 4, 2, BLOCK, LANES), bf16),
            pltpu.VMEM((SIDE, 4, 2, BLOCK, LANES), bf16),
            pltpu.VMEM((CHUNKS, SIDE - 1, SIDE, BLOCK, LANES), bf16),
            pltpu.VMEM((CHUNKS, SIDE, SIDE, BLOCK, LANES), bf16),
            pltpu.VMEM((GRID * BLOCK, LANES), jnp.float32),
            pltpu.VMEM((CHUNKS, MEM // 2, 2, rows, LAT_PAD), bf16),
            pltpu.VMEM((CHUNKS, MEM, rows, LAT_PAD), bf16),
            dma((5,)), dma((len(PIECES),)), dma((len(PIECES),)), dma((CHUNKS,)), dma((CHUNKS,)), dma((CHUNKS,)),
            dma((len(PIECES),)), dma((CHUNKS,)), dma((CHUNKS,)), dma((CHUNKS,)), dma((1,)), dma((1,)), dma((1,)),
        ],
        compiler_params=pltpu.CompilerParams(collective_id=0, has_side_effects=True, vmem_limit_bytes=60 * 1024 * 1024),
    )(jnp.transpose(control, (0, 2, 1, 3)), jnp.transpose(perturbation, (0, 2, 1, 3)), vertical,
      lat_counts.reshape(1, GRID), lon_counts.reshape(1, GRID))
    return jnp.transpose(summed.reshape(COLS, SHARE, LAT_PAD), (1, 0, 2))


def solution(mesh):
    in_specs = (P("mem", None, "grid", None), P("mem", None, "grid", None), P(), P(), P())
    out_specs = P("mem", "grid", None)
    return jax.shard_map(
        per_device, mesh=mesh, in_specs=in_specs, out_specs=out_specs, check_vma=False
    )
```

```python
import math

import jax
import jax.numpy as jnp
import numpy as np
from jax import lax
from jax.experimental import pallas as pl
from jax.experimental.pallas import tpu as pltpu
from jax.sharding import PartitionSpec as P

LAT = 361
LON = 720
LENGTH = 8
BAND = 48
MESH = pl.DeviceIdType.MESH
FAR = 20000.0
NORM = np.sqrt(np.sum(np.exp(np.float32(-2.0) * np.arange(BAND + 1, dtype=np.float32) / np.float32(LENGTH)), dtype=np.float32))
SCALE = float(np.float32(1.0) / NORM)

GRID = 64
SIDE = 8
MEM = 8
MEMBERS = 4
LEV = 32
ROWS = 6
COLS = 12
LON_PAD = GRID * COLS
LAT_PAD = GRID * ROWS
LANES = MEMBERS * LEV
CHUNK = 4
CHUNKS = COLS // CHUNK
PAIRS = ROWS // 2
BLOCK = CHUNK * ROWS
SHARE = LEV // MEM
TILE = 8
PIECES = ((1, 0, 3), (2, 0, 3))


def nt(a, b):
    return lax.dot_general(a, b, (((1,), (1,)), ((), ())), preferred_element_type=jnp.float32)


def iota(shape, dim):
    return lax.broadcasted_iota(jnp.int32, shape, dim)


def positions_down(counts, slab, place, missing):
    rows = slab.shape[0]
    devices = iota((rows, GRID), 1)
    table = jnp.broadcast_to(counts, (128, GRID)).astype(jnp.bfloat16)
    start = nt((devices < slab).astype(jnp.float32).astype(jnp.bfloat16), table)
    count = nt((devices == slab).astype(jnp.float32).astype(jnp.bfloat16), table)
    place = place.astype(jnp.float32)
    return jnp.where(place < count, start + place, missing)


def positions_across(counts, slab, place, missing):
    lanes = slab.shape[1]
    devices = iota((GRID, lanes), 0)
    table = jnp.broadcast_to(counts, (8, GRID)).astype(jnp.bfloat16)
    before = (devices < slab).astype(jnp.float32).astype(jnp.bfloat16)
    own = (devices == slab).astype(jnp.float32).astype(jnp.bfloat16)
    start = jnp.dot(table, before, preferred_element_type=jnp.float32)
    count = jnp.dot(table, own, preferred_element_type=jnp.float32)
    place = place.astype(jnp.float32)
    return jnp.where(place < count, start + place, missing)


def weights(lag, inside):
    return jnp.where(inside, jnp.exp(lag * (-1.0 / LENGTH)) * SCALE, 0.0).astype(jnp.bfloat16)


def interleave(first, second):
    low = iota(first.shape, 1) < 4
    even = jnp.where(low, first, pltpu.roll(second, 4, 1))
    odd = jnp.where(low, pltpu.roll(first, 4, 1), second)
    return even, odd


def kernel(control, perturbation, vertical, lat_counts, lon_counts, parts,
           ctrl, pert, vert, latc, lonc, lon_t, lat_k, send, column, middle, recv, wide, part,
           in_sem, mid_send_sem, mid_recv_sem, send_sem, recv_sem, own_sem, near_sem, psend_sem, precv_sem, pown_sem, col_send_sem, col_recv_sem, col_own_sem):
    me = lax.axis_index("grid")
    mine = lax.axis_index("mem")
    my_y, my_x, my_z = me // SIDE, (me % SIDE) // 2, me % 2

    def across(step):
        to_x, to_z = (my_x + step // 2) % 4, (my_z + step % 2) % 2
        return my_y * SIDE + to_x * 2 + to_z, to_x, to_z

    def along(step):
        to_y = (my_y + 4 + (step // 2) * (2 * (step % 2) - 1)) % SIDE
        return to_y * SIDE + me % SIDE, to_y

    barrier = pltpu.get_barrier_semaphore()

    def greet(step, carry):
        pl.semaphore_signal(barrier, inc=1, device_id={"grid": across(step)[0]}, device_id_type=MESH)
        pl.semaphore_signal(barrier, inc=1, device_id={"grid": along(step)[0]}, device_id_type=MESH)
        pl.semaphore_signal(barrier, inc=1, device_id={"mem": (mine + step) % MEM}, device_id_type=MESH)
        return carry

    lax.fori_loop(1, SIDE, greet, 0)

    loads = [pltpu.make_async_copy(source, target, in_sem.at[index]) for index, (source, target) in enumerate(
        ((lon_counts, lonc), (control, ctrl), (lat_counts, latc), (vertical, vert), (perturbation, pert)))]
    for load in loads:
        load.start()

    loads[0].wait()
    counts = lonc[...].astype(jnp.float32)
    lanes = iota((GRID, LON_PAD), 1)
    source = positions_across(counts, lanes // COLS, lanes[:8] % COLS, -FAR)
    def smooth_chunk(q):
        rows = iota((GRID * CHUNK, GRID), 0)
        place = iota((GRID * CHUNK, 128), 0) % CHUNK + q * CHUNK
        target = positions_down(counts, rows // CHUNK, place, FAR)
        for tile in range(LON_PAD // 128):
            lag = target - source[:1, tile * 128:(tile + 1) * 128]
            lag = jnp.where(lag < 0, lag + LON, lag)
            lon_t[q, :, tile * 128:(tile + 1) * 128] = weights(lag, lag <= BAND)
        if q == 0:
            loads[1].wait()
        fields = jnp.concatenate([ctrl[:, i].reshape(LANES, LON_PAD) for i in range(ROWS)], axis=0)
        smooth = nt(lon_t[q], fields)
        for pair in range(PAIRS):
            first, second = [smooth[:, (2 * pair + half) * LANES:(2 * pair + half + 1) * LANES].reshape(GRID * CHUNK // 8, 8, LANES)
                             for half in range(2)]
            for parity, block in enumerate(interleave(first, second)):
                send[q, :, :, parity, pair * TILE:(pair + 1) * TILE, :] = block.astype(jnp.bfloat16).reshape(SIDE, 4, TILE, LANES)

    def send_direct(q):
        def direct(step, carry):
            peer, to_y = along(step)
            pltpu.make_async_remote_copy(
                src_ref=send.at[q, to_y, my_x, my_z], dst_ref=recv.at[q, my_y, 0],
                send_sem=send_sem.at[q], recv_sem=recv_sem.at[q],
                device_id={"grid": peer}, device_id_type=MESH).start()
            return carry

        lax.fori_loop(1, SIDE, direct, 0)

    stay = pltpu.make_async_copy(send.at[0, my_y], column.at[my_y], own_sem.at[0])
    settle = pltpu.make_async_copy(column.at[:, my_x, my_z], recv.at[0, :, 0], col_own_sem.at[0])

    def send_column():
        def far(step, carry):
            peer, to_y = along(step)
            pltpu.make_async_remote_copy(
                src_ref=send.at[0, to_y], dst_ref=column.at[my_y],
                send_sem=col_send_sem.at[0], recv_sem=col_recv_sem.at[0],
                device_id={"grid": peer}, device_id_type=MESH).start()
            return carry

        lax.fori_loop(1, SIDE, far, 0)
        stay.start()

    def pass_column():
        stay.wait()
        pltpu.make_async_copy(column.at[pl.ds(0, SIDE - 1)], column.at[pl.ds(0, SIDE - 1)], col_recv_sem.at[0]).wait()

        def near(step, carry):
            peer, to_x, to_z = across(step)
            pltpu.make_async_remote_copy(
                src_ref=column.at[:, to_x, to_z], dst_ref=recv.at[0, :, step],
                send_sem=send_sem.at[0], recv_sem=recv_sem.at[0],
                device_id={"grid": peer}, device_id_type=MESH).start()
            return carry

        lax.fori_loop(1, SIDE, near, 0)
        settle.start()

    def send_piece(piece):
        q, group, groups = PIECES[piece]
        span = pl.ds(group * TILE, groups * TILE)

        def spread(step, carry):
            peer, to_x, to_z = across(step)
            pltpu.make_async_remote_copy(
                src_ref=send.at[q, :, to_x, to_z, span], dst_ref=middle.at[q, step - 1, :, span],
                send_sem=mid_send_sem.at[piece], recv_sem=mid_recv_sem.at[piece],
                device_id={"grid": peer}, device_id_type=MESH).start()
            return carry

        lax.fori_loop(1, SIDE, spread, 0)

    def keep(q):
        pltpu.make_async_copy(send.at[q, my_y, my_x, my_z], recv.at[q, my_y, 0], own_sem.at[q]).start()

    def pass_on(piece):
        q, group, groups = PIECES[piece]
        span = pl.ds(group * TILE, groups * TILE)
        pltpu.make_async_copy(middle.at[q, :, :, span], middle.at[q, :, :, span], mid_recv_sem.at[piece]).wait()

        def forward(step, carry):
            peer, to_y = along(step)
            pltpu.make_async_remote_copy(
                src_ref=middle.at[q, :, to_y, span], dst_ref=recv.at[q, my_y, pl.ds(1, SIDE - 1), span],
                send_sem=send_sem.at[q], recv_sem=recv_sem.at[q],
                device_id={"grid": peer}, device_id_type=MESH).start()
            return carry

        lax.fori_loop(1, SIDE, forward, 0)
        pltpu.make_async_copy(middle.at[q, :, my_y, span], recv.at[q, my_y, pl.ds(1, SIDE - 1), span], near_sem.at[piece]).start()

    smooth_chunk(0)
    pl.semaphore_wait(barrier, 3 * (SIDE - 1))
    send_column()
    smooth_chunk(1)
    send_piece(0)
    send_direct(1)
    smooth_chunk(2)
    send_piece(1)
    send_direct(2)
    for q in range(1, CHUNKS):
        keep(q)

    loads[2].wait()
    counts = latc[...].astype(jnp.float32)
    half_rows = GRID * PAIRS
    lanes = iota((GRID, LAT_PAD), 1)
    target = positions_across(counts, lanes // ROWS, lanes[:8] % ROWS, -FAR)
    block = iota((LAT_PAD, GRID), 0) % half_rows // PAIRS
    step = block % SIDE
    slab = block // SIDE * SIDE + (my_x + 4 - step // 2) % 4 * 2 + (my_z + 2 - step % 2) % 2
    long_rows = iota((LAT_PAD, 128), 0)
    place = 2 * (long_rows % PAIRS) + long_rows // half_rows
    source = positions_down(counts, slab, place, FAR)
    for tile in range(LAT_PAD // 128):
        lag = target[:1, tile * 128:(tile + 1) * 128] - source
        lat_k[:, tile * 128:(tile + 1) * 128] = weights(lag, (lag >= 0) & (lag <= BAND))

    loads[3].wait()
    spread_lanes = (iota((LEV, LANES), 0) == iota((LEV, LANES), 1) % LEV).astype(jnp.float32).astype(jnp.bfloat16)
    wide_factor = jnp.dot(vert[...], spread_lanes, preferred_element_type=jnp.float32)
    wide_factor = jnp.concatenate([wide_factor] * MEMBERS, axis=0)
    mixing = jnp.where(iota((LANES, LANES), 0) // LEV == iota((LANES, LANES), 1) // LEV, wide_factor, 0.0).astype(jnp.bfloat16)

    pass_on(0)
    pass_column()
    pass_on(1)

    loads[4].wait()
    for q in range(CHUNKS):
        if q == 0:
            settle.wait()
        else:
            pltpu.make_async_copy(send.at[q, my_y, my_x, my_z], recv.at[q, my_y, 0], own_sem.at[q]).wait()
        for piece, (chunk, group, groups) in enumerate(PIECES):
            if chunk == q:
                span = pl.ds(group * TILE, groups * TILE)
                pltpu.make_async_copy(middle.at[q, :, my_y, span], recv.at[q, my_y, pl.ds(1, SIDE - 1), span], near_sem.at[piece]).wait()
        pltpu.make_async_copy(recv.at[q, pl.ds(0, SIDE - 1)], recv.at[q, pl.ds(0, SIDE - 1)], recv_sem.at[q]).wait()
        wide[...] = recv[q].astype(jnp.float32).reshape(GRID * BLOCK, LANES)
        mixed = []
        for c in range(CHUNK):
            fields = jnp.concatenate([wide[pl.ds(half * CHUNK + c, half_rows, stride=2 * CHUNK), :] for half in range(2)], axis=0)
            mixed.append(nt(mixing, fields.astype(jnp.bfloat16)).astype(jnp.bfloat16))
        filtered = jnp.dot(jnp.concatenate(mixed, axis=0), lat_k[...], preferred_element_type=jnp.float32)
        sums = []
        for c in range(CHUNK):
            field = filtered[c * LANES:(c + 1) * LANES].reshape(MEMBERS, LEV, LAT_PAD)
            sums.append(jnp.sum(field * pert[:, q * CHUNK + c].astype(jnp.float32), axis=0).reshape(LEV // 8, 8, LAT_PAD))
        for c in range(CHUNK):
            part[q, :, :, c] = sums[c].reshape(MEM // 2, 2, SHARE, LAT_PAD).astype(jnp.bfloat16)
        span = pl.ds(q * CHUNK, CHUNK)
        for step in (4, 3, 5, 2, 6, 1, 7):
            peer = (mine + step) % MEM
            pltpu.make_async_remote_copy(
                src_ref=part.at[q, peer // 2, peer % 2], dst_ref=parts.at[mine, span],
                send_sem=psend_sem.at[q], recv_sem=precv_sem.at[q],
                device_id={"mem": peer}, device_id_type=MESH).start()
        pltpu.make_async_copy(part.at[q, mine // 2, mine % 2], parts.at[mine, span], pown_sem.at[q]).start()

    pltpu.make_async_copy(column.at[pl.ds(0, SIDE - 1)], column.at[pl.ds(0, SIDE - 1)], col_send_sem.at[0]).wait()
    for piece, (q, group, groups) in enumerate(PIECES):
        span = pl.ds(group * TILE, groups * TILE)
        pltpu.make_async_copy(middle.at[q, :, :, span], middle.at[q, :, :, span], mid_send_sem.at[piece]).wait()
    for q in range(CHUNKS):
        pltpu.make_async_copy(recv.at[q, pl.ds(0, SIDE - 1)], recv.at[q, pl.ds(0, SIDE - 1)], send_sem.at[q]).wait()
        span = pl.ds(q * CHUNK, CHUNK)
        others = parts.at[pl.ds(0, MEM - 1), span]
        pltpu.make_async_copy(others, others, psend_sem.at[q]).wait()
        pltpu.make_async_copy(part.at[q, mine // 2, mine % 2], parts.at[mine, span], pown_sem.at[q]).wait()
        pltpu.make_async_copy(others, others, precv_sem.at[q]).wait()


def per_device(control, perturbation, vertical, lat_counts, lon_counts):
    bf16 = jnp.bfloat16
    dma = pltpu.SemaphoreType.DMA
    shares = pl.pallas_call(
        kernel,
        out_shape=jax.ShapeDtypeStruct((MEM, COLS, SHARE, LAT_PAD), bf16),
        in_specs=[pl.BlockSpec(memory_space=pltpu.HBM)] * 5,
        out_specs=pl.BlockSpec(memory_space=pltpu.HBM),
        scratch_shapes=[
            pltpu.VMEM((MEMBERS, ROWS, LEV, LON_PAD), bf16),
            pltpu.VMEM((MEMBERS, COLS, LEV, LAT_PAD), bf16),
            pltpu.VMEM((LEV, LEV), bf16),
            pltpu.VMEM((1, GRID), jnp.int32),
            pltpu.VMEM((1, GRID), jnp.int32),
            pltpu.VMEM((CHUNKS, GRID * CHUNK, LON_PAD), bf16),
            pltpu.VMEM((LAT_PAD, LAT_PAD), bf16),
            pltpu.VMEM((CHUNKS, SIDE, 4, 2, BLOCK, LANES), bf16),
            pltpu.VMEM((SIDE, 4, 2, BLOCK, LANES), bf16),
            pltpu.VMEM((CHUNKS, SIDE - 1, SIDE, BLOCK, LANES), bf16),
            pltpu.VMEM((CHUNKS, SIDE, SIDE, BLOCK, LANES), bf16),
            pltpu.VMEM((GRID * BLOCK, LANES), jnp.float32),
            pltpu.VMEM((CHUNKS, MEM // 2, 2, CHUNK, SHARE, LAT_PAD), bf16),
            dma((5,)), dma((len(PIECES),)), dma((len(PIECES),)), dma((CHUNKS,)), dma((CHUNKS,)), dma((CHUNKS,)),
            dma((len(PIECES),)), dma((CHUNKS,)), dma((CHUNKS,)), dma((CHUNKS,)), dma((1,)), dma((1,)), dma((1,)),
        ],
        compiler_params=pltpu.CompilerParams(collective_id=0, has_side_effects=True, vmem_limit_bytes=60 * 1024 * 1024),
    )(jnp.transpose(control, (0, 2, 1, 3)), jnp.transpose(perturbation, (0, 2, 1, 3)), vertical,
      lat_counts.reshape(1, GRID), lon_counts.reshape(1, GRID))
    return jnp.transpose(jnp.sum(shares.astype(jnp.float32), axis=0), (1, 0, 2))


def solution(mesh):
    in_specs = (P("mem", None, "grid", None), P("mem", None, "grid", None), P(), P(), P())
    out_specs = P("mem", "grid", None)
    return jax.shard_map(
        per_device, mesh=mesh, in_specs=in_specs, out_specs=out_specs, check_vma=False
    )
```

```python
import math

import jax
import jax.numpy as jnp
import numpy as np
from jax import lax
from jax.experimental import pallas as pl
from jax.experimental.pallas import tpu as pltpu
from jax.sharding import PartitionSpec as P

LAT = 361
LON = 720
LENGTH = 8
BAND = 48
MESH = pl.DeviceIdType.MESH
FAR = 20000.0
NORM = np.sqrt(np.sum(np.exp(np.float32(-2.0) * np.arange(BAND + 1, dtype=np.float32) / np.float32(LENGTH)), dtype=np.float32))
SCALE = float(np.float32(1.0) / NORM)

GRID = 64
SIDE = 8
MEM = 8
MEMBERS = 4
LEV = 32
ROWS = 6
COLS = 12
LON_PAD = GRID * COLS
LAT_PAD = GRID * ROWS
LANES = MEMBERS * LEV
CHUNK = 4
CHUNKS = COLS // CHUNK
PAIRS = ROWS // 2
BLOCK = CHUNK * ROWS
SHARE = LEV // MEM
TILE = 8
PIECES = ((1, 0, 1), (1, 1, 2), (2, 0, 3))


def nt(a, b):
    return lax.dot_general(a, b, (((1,), (1,)), ((), ())), preferred_element_type=jnp.float32)


def iota(shape, dim):
    return lax.broadcasted_iota(jnp.int32, shape, dim)


def positions_down(counts, slab, place, missing):
    rows = slab.shape[0]
    devices = iota((rows, GRID), 1)
    table = jnp.broadcast_to(counts, (128, GRID)).astype(jnp.bfloat16)
    start = nt((devices < slab).astype(jnp.float32).astype(jnp.bfloat16), table)
    count = nt((devices == slab).astype(jnp.float32).astype(jnp.bfloat16), table)
    place = place.astype(jnp.float32)
    return jnp.where(place < count, start + place, missing)


def positions_across(counts, slab, place, missing):
    lanes = slab.shape[1]
    devices = iota((GRID, lanes), 0)
    table = jnp.broadcast_to(counts, (8, GRID)).astype(jnp.bfloat16)
    before = (devices < slab).astype(jnp.float32).astype(jnp.bfloat16)
    own = (devices == slab).astype(jnp.float32).astype(jnp.bfloat16)
    start = jnp.dot(table, before, preferred_element_type=jnp.float32)
    count = jnp.dot(table, own, preferred_element_type=jnp.float32)
    place = place.astype(jnp.float32)
    return jnp.where(place < count, start + place, missing)


def weights(lag, inside):
    return jnp.where(inside, jnp.exp(lag * (-1.0 / LENGTH)) * SCALE, 0.0).astype(jnp.bfloat16)


def interleave(first, second):
    low = iota(first.shape, 1) < 4
    even = jnp.where(low, first, pltpu.roll(second, 4, 1))
    odd = jnp.where(low, pltpu.roll(first, 4, 1), second)
    return even, odd


def kernel(control, perturbation, vertical, lat_counts, lon_counts, parts,
           ctrl, pert, vert, latc, lonc, lon_t, lat_k, send, column, middle, recv, wide, part,
           in_sem, mid_send_sem, mid_recv_sem, send_sem, recv_sem, own_sem, near_sem, psend_sem, precv_sem, pown_sem, col_send_sem, col_recv_sem, col_own_sem):
    me = lax.axis_index("grid")
    mine = lax.axis_index("mem")
    my_y, my_x, my_z = me // SIDE, (me % SIDE) // 2, me % 2

    def across(step):
        to_x, to_z = (my_x + step // 2) % 4, (my_z + step % 2) % 2
        return my_y * SIDE + to_x * 2 + to_z, to_x, to_z

    def along(step):
        to_y = (my_y + 4 + (step // 2) * (2 * (step % 2) - 1)) % SIDE
        return to_y * SIDE + me % SIDE, to_y

    barrier = pltpu.get_barrier_semaphore()

    def greet(step, carry):
        pl.semaphore_signal(barrier, inc=1, device_id={"grid": across(step)[0]}, device_id_type=MESH)
        pl.semaphore_signal(barrier, inc=1, device_id={"grid": along(step)[0]}, device_id_type=MESH)
        pl.semaphore_signal(barrier, inc=1, device_id={"mem": (mine + step) % MEM}, device_id_type=MESH)
        return carry

    lax.fori_loop(1, SIDE, greet, 0)

    loads = [pltpu.make_async_copy(source, target, in_sem.at[index]) for index, (source, target) in enumerate(
        ((lon_counts, lonc), (control, ctrl), (lat_counts, latc), (vertical, vert), (perturbation, pert)))]
    for load in loads:
        load.start()

    loads[0].wait()
    counts = lonc[...].astype(jnp.float32)
    lanes = iota((GRID, LON_PAD), 1)
    source = positions_across(counts, lanes // COLS, lanes[:8] % COLS, -FAR)
    def smooth_chunk(q):
        rows = iota((GRID * CHUNK, GRID), 0)
        place = iota((GRID * CHUNK, 128), 0) % CHUNK + q * CHUNK
        target = positions_down(counts, rows // CHUNK, place, FAR)
        for tile in range(LON_PAD // 128):
            lag = target - source[:1, tile * 128:(tile + 1) * 128]
            lag = jnp.where(lag < 0, lag + LON, lag)
            lon_t[q, :, tile * 128:(tile + 1) * 128] = weights(lag, lag <= BAND)
        if q == 0:
            loads[1].wait()
        fields = jnp.concatenate([ctrl[:, i].reshape(LANES, LON_PAD) for i in range(ROWS)], axis=0)
        smooth = nt(lon_t[q], fields)
        for pair in range(PAIRS):
            first, second = [smooth[:, (2 * pair + half) * LANES:(2 * pair + half + 1) * LANES].reshape(GRID * CHUNK // 8, 8, LANES)
                             for half in range(2)]
            for parity, block in enumerate(interleave(first, second)):
                send[q, :, :, parity, pair * TILE:(pair + 1) * TILE, :] = block.astype(jnp.bfloat16).reshape(SIDE, 4, TILE, LANES)

    def send_direct(q):
        def direct(step, carry):
            peer, to_y = along(step)
            pltpu.make_async_remote_copy(
                src_ref=send.at[q, to_y, my_x, my_z], dst_ref=recv.at[q, my_y, 0],
                send_sem=send_sem.at[q], recv_sem=recv_sem.at[q],
                device_id={"grid": peer}, device_id_type=MESH).start()
            return carry

        lax.fori_loop(1, SIDE, direct, 0)

    stay = pltpu.make_async_copy(send.at[0, my_y], column.at[my_y], own_sem.at[0])
    settle = pltpu.make_async_copy(column.at[:, my_x, my_z], recv.at[0, :, 0], col_own_sem.at[0])

    def send_column():
        def far(step, carry):
            peer, to_y = along(step)
            pltpu.make_async_remote_copy(
                src_ref=send.at[0, to_y], dst_ref=column.at[my_y],
                send_sem=col_send_sem.at[0], recv_sem=col_recv_sem.at[0],
                device_id={"grid": peer}, device_id_type=MESH).start()
            return carry

        lax.fori_loop(1, SIDE, far, 0)
        stay.start()

    def pass_column():
        stay.wait()
        pltpu.make_async_copy(column.at[pl.ds(0, SIDE - 1)], column.at[pl.ds(0, SIDE - 1)], col_recv_sem.at[0]).wait()

        def near(step, carry):
            peer, to_x, to_z = across(step)
            pltpu.make_async_remote_copy(
                src_ref=column.at[:, to_x, to_z], dst_ref=recv.at[0, :, step],
                send_sem=send_sem.at[0], recv_sem=recv_sem.at[0],
                device_id={"grid": peer}, device_id_type=MESH).start()
            return carry

        lax.fori_loop(1, SIDE, near, 0)
        settle.start()

    def send_piece(piece):
        q, group, groups = PIECES[piece]
        span = pl.ds(group * TILE, groups * TILE)

        def spread(step, carry):
            peer, to_x, to_z = across(step)
            pltpu.make_async_remote_copy(
                src_ref=send.at[q, :, to_x, to_z, span], dst_ref=middle.at[q, step - 1, :, span],
                send_sem=mid_send_sem.at[piece], recv_sem=mid_recv_sem.at[piece],
                device_id={"grid": peer}, device_id_type=MESH).start()
            return carry

        lax.fori_loop(1, SIDE, spread, 0)

    def keep(q):
        pltpu.make_async_copy(send.at[q, my_y, my_x, my_z], recv.at[q, my_y, 0], own_sem.at[q]).start()

    def pass_on(piece):
        q, group, groups = PIECES[piece]
        span = pl.ds(group * TILE, groups * TILE)
        pltpu.make_async_copy(middle.at[q, :, :, span], middle.at[q, :, :, span], mid_recv_sem.at[piece]).wait()

        def forward(step, carry):
            peer, to_y = along(step)
            pltpu.make_async_remote_copy(
                src_ref=middle.at[q, :, to_y, span], dst_ref=recv.at[q, my_y, pl.ds(1, SIDE - 1), span],
                send_sem=send_sem.at[q], recv_sem=recv_sem.at[q],
                device_id={"grid": peer}, device_id_type=MESH).start()
            return carry

        lax.fori_loop(1, SIDE, forward, 0)
        pltpu.make_async_copy(middle.at[q, :, my_y, span], recv.at[q, my_y, pl.ds(1, SIDE - 1), span], near_sem.at[piece]).start()

    smooth_chunk(0)
    pl.semaphore_wait(barrier, 3 * (SIDE - 1))
    send_column()
    smooth_chunk(1)
    send_piece(0)
    send_piece(1)
    send_direct(1)
    smooth_chunk(2)
    send_piece(2)
    send_direct(2)
    for q in range(1, CHUNKS):
        keep(q)

    loads[2].wait()
    counts = latc[...].astype(jnp.float32)
    half_rows = GRID * PAIRS
    lanes = iota((GRID, LAT_PAD), 1)
    target = positions_across(counts, lanes // ROWS, lanes[:8] % ROWS, -FAR)
    block = iota((LAT_PAD, GRID), 0) % half_rows // PAIRS
    step = block % SIDE
    slab = block // SIDE * SIDE + (my_x + 4 - step // 2) % 4 * 2 + (my_z + 2 - step % 2) % 2
    long_rows = iota((LAT_PAD, 128), 0)
    place = 2 * (long_rows % PAIRS) + long_rows // half_rows
    source = positions_down(counts, slab, place, FAR)
    for tile in range(LAT_PAD // 128):
        lag = target[:1, tile * 128:(tile + 1) * 128] - source
        lat_k[:, tile * 128:(tile + 1) * 128] = weights(lag, (lag >= 0) & (lag <= BAND))

    loads[3].wait()
    spread_lanes = (iota((LEV, LANES), 0) == iota((LEV, LANES), 1) % LEV).astype(jnp.float32).astype(jnp.bfloat16)
    wide_factor = jnp.dot(vert[...], spread_lanes, preferred_element_type=jnp.float32)
    wide_factor = jnp.concatenate([wide_factor] * MEMBERS, axis=0)
    mixing = jnp.where(iota((LANES, LANES), 0) // LEV == iota((LANES, LANES), 1) // LEV, wide_factor, 0.0).astype(jnp.bfloat16)

    pass_on(0)
    pass_on(1)
    pass_column()
    pass_on(2)

    loads[4].wait()
    for q in range(CHUNKS):
        if q == 0:
            settle.wait()
        else:
            pltpu.make_async_copy(send.at[q, my_y, my_x, my_z], recv.at[q, my_y, 0], own_sem.at[q]).wait()
        for piece, (chunk, group, groups) in enumerate(PIECES):
            if chunk == q:
                span = pl.ds(group * TILE, groups * TILE)
                pltpu.make_async_copy(middle.at[q, :, my_y, span], recv.at[q, my_y, pl.ds(1, SIDE - 1), span], near_sem.at[piece]).wait()
        pltpu.make_async_copy(recv.at[q, pl.ds(0, SIDE - 1)], recv.at[q, pl.ds(0, SIDE - 1)], recv_sem.at[q]).wait()
        wide[...] = recv[q].astype(jnp.float32).reshape(GRID * BLOCK, LANES)
        mixed = []
        for c in range(CHUNK):
            fields = jnp.concatenate([wide[pl.ds(half * CHUNK + c, half_rows, stride=2 * CHUNK), :] for half in range(2)], axis=0)
            mixed.append(nt(mixing, fields.astype(jnp.bfloat16)).astype(jnp.bfloat16))
        filtered = jnp.dot(jnp.concatenate(mixed, axis=0), lat_k[...], preferred_element_type=jnp.float32)
        sums = []
        for c in range(CHUNK):
            field = filtered[c * LANES:(c + 1) * LANES].reshape(MEMBERS, LEV, LAT_PAD)
            sums.append(jnp.sum(field * pert[:, q * CHUNK + c].astype(jnp.float32), axis=0).reshape(LEV // 8, 8, LAT_PAD))
        for c in range(CHUNK):
            part[q, :, :, c] = sums[c].reshape(MEM // 2, 2, SHARE, LAT_PAD).astype(jnp.bfloat16)
        span = pl.ds(q * CHUNK, CHUNK)
        for step in (4, 3, 5, 2, 6, 1, 7):
            peer = (mine + step) % MEM
            pltpu.make_async_remote_copy(
                src_ref=part.at[q, peer // 2, peer % 2], dst_ref=parts.at[mine, span],
                send_sem=psend_sem.at[q], recv_sem=precv_sem.at[q],
                device_id={"mem": peer}, device_id_type=MESH).start()
        pltpu.make_async_copy(part.at[q, mine // 2, mine % 2], parts.at[mine, span], pown_sem.at[q]).start()

    pltpu.make_async_copy(column.at[pl.ds(0, SIDE - 1)], column.at[pl.ds(0, SIDE - 1)], col_send_sem.at[0]).wait()
    for piece, (q, group, groups) in enumerate(PIECES):
        span = pl.ds(group * TILE, groups * TILE)
        pltpu.make_async_copy(middle.at[q, :, :, span], middle.at[q, :, :, span], mid_send_sem.at[piece]).wait()
    for q in range(CHUNKS):
        pltpu.make_async_copy(recv.at[q, pl.ds(0, SIDE - 1)], recv.at[q, pl.ds(0, SIDE - 1)], send_sem.at[q]).wait()
        span = pl.ds(q * CHUNK, CHUNK)
        others = parts.at[pl.ds(0, MEM - 1), span]
        pltpu.make_async_copy(others, others, psend_sem.at[q]).wait()
        pltpu.make_async_copy(part.at[q, mine // 2, mine % 2], parts.at[mine, span], pown_sem.at[q]).wait()
        pltpu.make_async_copy(others, others, precv_sem.at[q]).wait()


def per_device(control, perturbation, vertical, lat_counts, lon_counts):
    bf16 = jnp.bfloat16
    dma = pltpu.SemaphoreType.DMA
    shares = pl.pallas_call(
        kernel,
        out_shape=jax.ShapeDtypeStruct((MEM, COLS, SHARE, LAT_PAD), bf16),
        in_specs=[pl.BlockSpec(memory_space=pltpu.HBM)] * 5,
        out_specs=pl.BlockSpec(memory_space=pltpu.HBM),
        scratch_shapes=[
            pltpu.VMEM((MEMBERS, ROWS, LEV, LON_PAD), bf16),
            pltpu.VMEM((MEMBERS, COLS, LEV, LAT_PAD), bf16),
            pltpu.VMEM((LEV, LEV), bf16),
            pltpu.VMEM((1, GRID), jnp.int32),
            pltpu.VMEM((1, GRID), jnp.int32),
            pltpu.VMEM((CHUNKS, GRID * CHUNK, LON_PAD), bf16),
            pltpu.VMEM((LAT_PAD, LAT_PAD), bf16),
            pltpu.VMEM((CHUNKS, SIDE, 4, 2, BLOCK, LANES), bf16),
            pltpu.VMEM((SIDE, 4, 2, BLOCK, LANES), bf16),
            pltpu.VMEM((CHUNKS, SIDE - 1, SIDE, BLOCK, LANES), bf16),
            pltpu.VMEM((CHUNKS, SIDE, SIDE, BLOCK, LANES), bf16),
            pltpu.VMEM((GRID * BLOCK, LANES), jnp.float32),
            pltpu.VMEM((CHUNKS, MEM // 2, 2, CHUNK, SHARE, LAT_PAD), bf16),
            dma((5,)), dma((len(PIECES),)), dma((len(PIECES),)), dma((CHUNKS,)), dma((CHUNKS,)), dma((CHUNKS,)),
            dma((len(PIECES),)), dma((CHUNKS,)), dma((CHUNKS,)), dma((CHUNKS,)), dma((1,)), dma((1,)), dma((1,)),
        ],
        compiler_params=pltpu.CompilerParams(collective_id=0, has_side_effects=True, vmem_limit_bytes=60 * 1024 * 1024),
    )(jnp.transpose(control, (0, 2, 1, 3)), jnp.transpose(perturbation, (0, 2, 1, 3)), vertical,
      lat_counts.reshape(1, GRID), lon_counts.reshape(1, GRID))
    return jnp.transpose(jnp.sum(shares.astype(jnp.float32), axis=0), (1, 0, 2))


def solution(mesh):
    in_specs = (P("mem", None, "grid", None), P("mem", None, "grid", None), P(), P(), P())
    out_specs = P("mem", "grid", None)
    return jax.shard_map(
        per_device, mesh=mesh, in_specs=in_specs, out_specs=out_specs, check_vma=False
    )
```

```python
import math

import jax
import jax.numpy as jnp
import numpy as np
from jax import lax
from jax.experimental import pallas as pl
from jax.experimental.pallas import tpu as pltpu
from jax.sharding import PartitionSpec as P

LAT = 361
LON = 720
LENGTH = 8
BAND = 48
MESH = pl.DeviceIdType.MESH
FAR = 20000.0
NORM = np.sqrt(np.sum(np.exp(np.float32(-2.0) * np.arange(BAND + 1, dtype=np.float32) / np.float32(LENGTH)), dtype=np.float32))
SCALE = float(np.float32(1.0) / NORM)

GRID = 64
SIDE = 8
MEM = 8
MEMBERS = 4
LEV = 32
ROWS = 6
COLS = 12
LON_PAD = GRID * COLS
LAT_PAD = GRID * ROWS
LANES = MEMBERS * LEV
CHUNK = 4
CHUNKS = COLS // CHUNK
PAIRS = ROWS // 2
BLOCK = CHUNK * ROWS
SHARE = LEV // MEM
TILE = 8
PIECES = ((1, 0, 3), (2, 0, 3))


def nt(a, b):
    return lax.dot_general(a, b, (((1,), (1,)), ((), ())), preferred_element_type=jnp.float32)


def iota(shape, dim):
    return lax.broadcasted_iota(jnp.int32, shape, dim)


def positions_down(counts, slab, place, missing):
    rows = slab.shape[0]
    devices = iota((rows, GRID), 1)
    table = jnp.broadcast_to(counts, (128, GRID)).astype(jnp.bfloat16)
    start = nt((devices < slab).astype(jnp.float32).astype(jnp.bfloat16), table)
    count = nt((devices == slab).astype(jnp.float32).astype(jnp.bfloat16), table)
    place = place.astype(jnp.float32)
    return jnp.where(place < count, start + place, missing)


def positions_across(counts, slab, place, missing):
    lanes = slab.shape[1]
    devices = iota((GRID, lanes), 0)
    table = jnp.broadcast_to(counts, (8, GRID)).astype(jnp.bfloat16)
    before = (devices < slab).astype(jnp.float32).astype(jnp.bfloat16)
    own = (devices == slab).astype(jnp.float32).astype(jnp.bfloat16)
    start = jnp.dot(table, before, preferred_element_type=jnp.float32)
    count = jnp.dot(table, own, preferred_element_type=jnp.float32)
    place = place.astype(jnp.float32)
    return jnp.where(place < count, start + place, missing)


def weights(lag, inside):
    return jnp.where(inside, jnp.exp(lag * (-1.0 / LENGTH)) * SCALE, 0.0).astype(jnp.bfloat16)


def interleave(first, second):
    low = iota(first.shape, 1) < 4
    even = jnp.where(low, first, pltpu.roll(second, 4, 1))
    odd = jnp.where(low, pltpu.roll(first, 4, 1), second)
    return even, odd


def kernel(control, perturbation, vertical, lat_counts, lon_counts, parts,
           ctrl, pert, vert, latc, lonc, lon_t, lat_k, send, column, middle, recv, wide, part,
           in_sem, mid_send_sem, mid_recv_sem, send_sem, recv_sem, own_sem, near_sem, psend_sem, precv_sem, pown_sem, col_send_sem, col_recv_sem, col_own_sem, dir_send_sem, dir_recv_sem):
    me = lax.axis_index("grid")
    mine = lax.axis_index("mem")
    my_y, my_x, my_z = me // SIDE, (me % SIDE) // 2, me % 2

    def across(step):
        to_x, to_z = (my_x + step // 2) % 4, (my_z + step % 2) % 2
        return my_y * SIDE + to_x * 2 + to_z, to_x, to_z

    def along(step):
        to_y = (my_y + 4 + (step // 2) * (2 * (step % 2) - 1)) % SIDE
        return to_y * SIDE + me % SIDE, to_y

    barrier = pltpu.get_barrier_semaphore()

    def greet(step, carry):
        pl.semaphore_signal(barrier, inc=1, device_id={"grid": across(step)[0]}, device_id_type=MESH)
        pl.semaphore_signal(barrier, inc=1, device_id={"grid": along(step)[0]}, device_id_type=MESH)
        pl.semaphore_signal(barrier, inc=1, device_id={"mem": (mine + step) % MEM}, device_id_type=MESH)
        return carry

    lax.fori_loop(1, SIDE, greet, 0)

    loads = [pltpu.make_async_copy(source, target, in_sem.at[index]) for index, (source, target) in enumerate(
        ((lon_counts, lonc), (control, ctrl), (lat_counts, latc), (vertical, vert), (perturbation, pert)))]
    for load in loads:
        load.start()

    loads[0].wait()
    counts = lonc[...].astype(jnp.float32)
    lanes = iota((GRID, LON_PAD), 1)
    source = positions_across(counts, lanes // COLS, lanes[:8] % COLS, -FAR)
    def smooth_chunk(q):
        rows = iota((GRID * CHUNK, GRID), 0)
        place = iota((GRID * CHUNK, 128), 0) % CHUNK + q * CHUNK
        target = positions_down(counts, rows // CHUNK, place, FAR)
        for tile in range(LON_PAD // 128):
            lag = target - source[:1, tile * 128:(tile + 1) * 128]
            lag = jnp.where(lag < 0, lag + LON, lag)
            lon_t[q, :, tile * 128:(tile + 1) * 128] = weights(lag, lag <= BAND)
        if q == 0:
            loads[1].wait()
        fields = jnp.concatenate([ctrl[:, i].reshape(LANES, LON_PAD) for i in range(ROWS)], axis=0)
        smooth = nt(lon_t[q], fields)
        for pair in range(PAIRS):
            first, second = [smooth[:, (2 * pair + half) * LANES:(2 * pair + half + 1) * LANES].reshape(GRID * CHUNK // 8, 8, LANES)
                             for half in range(2)]
            for parity, block in enumerate(interleave(first, second)):
                send[q, :, :, parity, pair * TILE:(pair + 1) * TILE, :] = block.astype(jnp.bfloat16).reshape(SIDE, 4, TILE, LANES)

    later = pl.ds(1, CHUNKS - 1)

    def send_direct():
        def direct(step, carry):
            peer, to_y = along(step)
            pltpu.make_async_remote_copy(
                src_ref=send.at[later, to_y, my_x, my_z], dst_ref=recv.at[later, my_y, 0],
                send_sem=dir_send_sem.at[0], recv_sem=dir_recv_sem.at[0],
                device_id={"grid": peer}, device_id_type=MESH).start()
            return carry

        lax.fori_loop(1, SIDE, direct, 0)

    stay = pltpu.make_async_copy(send.at[0, my_y], column.at[my_y], own_sem.at[0])
    settle = pltpu.make_async_copy(column.at[:, my_x, my_z], recv.at[0, :, 0], col_own_sem.at[0])

    def send_column():
        def far(step, carry):
            peer, to_y = along(step)
            pltpu.make_async_remote_copy(
                src_ref=send.at[0, to_y], dst_ref=column.at[my_y],
                send_sem=col_send_sem.at[0], recv_sem=col_recv_sem.at[0],
                device_id={"grid": peer}, device_id_type=MESH).start()
            return carry

        lax.fori_loop(1, SIDE, far, 0)
        stay.start()

    def pass_column():
        stay.wait()
        pltpu.make_async_copy(column.at[pl.ds(0, SIDE - 1)], column.at[pl.ds(0, SIDE - 1)], col_recv_sem.at[0]).wait()

        def near(step, carry):
            peer, to_x, to_z = across(step)
            pltpu.make_async_remote_copy(
                src_ref=column.at[:, to_x, to_z], dst_ref=recv.at[0, :, step],
                send_sem=send_sem.at[0], recv_sem=recv_sem.at[0],
                device_id={"grid": peer}, device_id_type=MESH).start()
            return carry

        lax.fori_loop(1, SIDE, near, 0)
        settle.start()

    def send_piece(piece):
        q, group, groups = PIECES[piece]
        span = pl.ds(group * TILE, groups * TILE)

        def spread(step, carry):
            peer, to_x, to_z = across(step)
            pltpu.make_async_remote_copy(
                src_ref=send.at[q, :, to_x, to_z, span], dst_ref=middle.at[q, step - 1, :, span],
                send_sem=mid_send_sem.at[piece], recv_sem=mid_recv_sem.at[piece],
                device_id={"grid": peer}, device_id_type=MESH).start()
            return carry

        lax.fori_loop(1, SIDE, spread, 0)

    def keep(q):
        pltpu.make_async_copy(send.at[q, my_y, my_x, my_z], recv.at[q, my_y, 0], own_sem.at[q]).start()

    def pass_on(piece):
        q, group, groups = PIECES[piece]
        span = pl.ds(group * TILE, groups * TILE)
        pltpu.make_async_copy(middle.at[q, :, :, span], middle.at[q, :, :, span], mid_recv_sem.at[piece]).wait()

        def forward(step, carry):
            peer, to_y = along(step)
            pltpu.make_async_remote_copy(
                src_ref=middle.at[q, :, to_y, span], dst_ref=recv.at[q, my_y, pl.ds(1, SIDE - 1), span],
                send_sem=send_sem.at[q], recv_sem=recv_sem.at[q],
                device_id={"grid": peer}, device_id_type=MESH).start()
            return carry

        lax.fori_loop(1, SIDE, forward, 0)
        pltpu.make_async_copy(middle.at[q, :, my_y, span], recv.at[q, my_y, pl.ds(1, SIDE - 1), span], near_sem.at[piece]).start()

    smooth_chunk(0)
    pl.semaphore_wait(barrier, 3 * (SIDE - 1))
    send_column()
    smooth_chunk(1)
    send_piece(0)
    smooth_chunk(2)
    send_piece(1)
    send_direct()
    for q in range(1, CHUNKS):
        keep(q)

    loads[2].wait()
    counts = latc[...].astype(jnp.float32)
    half_rows = GRID * PAIRS
    lanes = iota((GRID, LAT_PAD), 1)
    target = positions_across(counts, lanes // ROWS, lanes[:8] % ROWS, -FAR)
    block = iota((LAT_PAD, GRID), 0) % half_rows // PAIRS
    step = block % SIDE
    slab = block // SIDE * SIDE + (my_x + 4 - step // 2) % 4 * 2 + (my_z + 2 - step % 2) % 2
    long_rows = iota((LAT_PAD, 128), 0)
    place = 2 * (long_rows % PAIRS) + long_rows // half_rows
    source = positions_down(counts, slab, place, FAR)
    for tile in range(LAT_PAD // 128):
        lag = target[:1, tile * 128:(tile + 1) * 128] - source
        lat_k[:, tile * 128:(tile + 1) * 128] = weights(lag, (lag >= 0) & (lag <= BAND))

    loads[3].wait()
    spread_lanes = (iota((LEV, LANES), 0) == iota((LEV, LANES), 1) % LEV).astype(jnp.float32).astype(jnp.bfloat16)
    wide_factor = jnp.dot(vert[...], spread_lanes, preferred_element_type=jnp.float32)
    wide_factor = jnp.concatenate([wide_factor] * MEMBERS, axis=0)
    mixing = jnp.where(iota((LANES, LANES), 0) // LEV == iota((LANES, LANES), 1) // LEV, wide_factor, 0.0).astype(jnp.bfloat16)

    pass_on(0)
    pass_column()
    pass_on(1)

    loads[4].wait()
    for q in range(CHUNKS):
        if q == 1:
            straight = recv.at[later, pl.ds(0, SIDE - 1), 0]
            pltpu.make_async_copy(straight, straight, dir_recv_sem.at[0]).wait()
        if q == 0:
            settle.wait()
        else:
            pltpu.make_async_copy(send.at[q, my_y, my_x, my_z], recv.at[q, my_y, 0], own_sem.at[q]).wait()
        for piece, (chunk, group, groups) in enumerate(PIECES):
            if chunk == q:
                span = pl.ds(group * TILE, groups * TILE)
                pltpu.make_async_copy(middle.at[q, :, my_y, span], recv.at[q, my_y, pl.ds(1, SIDE - 1), span], near_sem.at[piece]).wait()
        some = recv.at[q, pl.ds(0, SIDE - 1), pl.ds(0, SIDE if q == 0 else SIDE - 1)]
        pltpu.make_async_copy(some, some, recv_sem.at[q]).wait()
        wide[...] = recv[q].astype(jnp.float32).reshape(GRID * BLOCK, LANES)
        mixed = []
        for c in range(CHUNK):
            fields = jnp.concatenate([wide[pl.ds(half * CHUNK + c, half_rows, stride=2 * CHUNK), :] for half in range(2)], axis=0)
            mixed.append(nt(mixing, fields.astype(jnp.bfloat16)).astype(jnp.bfloat16))
        filtered = jnp.dot(jnp.concatenate(mixed, axis=0), lat_k[...], preferred_element_type=jnp.float32)
        sums = []
        for c in range(CHUNK):
            field = filtered[c * LANES:(c + 1) * LANES].reshape(MEMBERS, LEV, LAT_PAD)
            sums.append(jnp.sum(field * pert[:, q * CHUNK + c].astype(jnp.float32), axis=0).reshape(LEV // 8, 8, LAT_PAD))
        for c in range(CHUNK):
            part[q, :, :, c] = sums[c].reshape(MEM // 2, 2, SHARE, LAT_PAD).astype(jnp.bfloat16)
        span = pl.ds(q * CHUNK, CHUNK)
        for step in (4, 3, 5, 2, 6, 1, 7):
            peer = (mine + step) % MEM
            pltpu.make_async_remote_copy(
                src_ref=part.at[q, peer // 2, peer % 2], dst_ref=parts.at[mine, span],
                send_sem=psend_sem.at[q], recv_sem=precv_sem.at[q],
                device_id={"mem": peer}, device_id_type=MESH).start()
        pltpu.make_async_copy(part.at[q, mine // 2, mine % 2], parts.at[mine, span], pown_sem.at[q]).start()

    straight = recv.at[later, pl.ds(0, SIDE - 1), 0]
    pltpu.make_async_copy(straight, straight, dir_send_sem.at[0]).wait()
    pltpu.make_async_copy(column.at[pl.ds(0, SIDE - 1)], column.at[pl.ds(0, SIDE - 1)], col_send_sem.at[0]).wait()
    for piece, (q, group, groups) in enumerate(PIECES):
        span = pl.ds(group * TILE, groups * TILE)
        pltpu.make_async_copy(middle.at[q, :, :, span], middle.at[q, :, :, span], mid_send_sem.at[piece]).wait()
    for q in range(CHUNKS):
        some = recv.at[q, pl.ds(0, SIDE - 1), pl.ds(0, SIDE if q == 0 else SIDE - 1)]
        pltpu.make_async_copy(some, some, send_sem.at[q]).wait()
        span = pl.ds(q * CHUNK, CHUNK)
        others = parts.at[pl.ds(0, MEM - 1), span]
        pltpu.make_async_copy(others, others, psend_sem.at[q]).wait()
        pltpu.make_async_copy(part.at[q, mine // 2, mine % 2], parts.at[mine, span], pown_sem.at[q]).wait()
        pltpu.make_async_copy(others, others, precv_sem.at[q]).wait()


def per_device(control, perturbation, vertical, lat_counts, lon_counts):
    bf16 = jnp.bfloat16
    dma = pltpu.SemaphoreType.DMA
    shares = pl.pallas_call(
        kernel,
        out_shape=jax.ShapeDtypeStruct((MEM, COLS, SHARE, LAT_PAD), bf16),
        in_specs=[pl.BlockSpec(memory_space=pltpu.HBM)] * 5,
        out_specs=pl.BlockSpec(memory_space=pltpu.HBM),
        scratch_shapes=[
            pltpu.VMEM((MEMBERS, ROWS, LEV, LON_PAD), bf16),
            pltpu.VMEM((MEMBERS, COLS, LEV, LAT_PAD), bf16),
            pltpu.VMEM((LEV, LEV), bf16),
            pltpu.VMEM((1, GRID), jnp.int32),
            pltpu.VMEM((1, GRID), jnp.int32),
            pltpu.VMEM((CHUNKS, GRID * CHUNK, LON_PAD), bf16),
            pltpu.VMEM((LAT_PAD, LAT_PAD), bf16),
            pltpu.VMEM((CHUNKS, SIDE, 4, 2, BLOCK, LANES), bf16),
            pltpu.VMEM((SIDE, 4, 2, BLOCK, LANES), bf16),
            pltpu.VMEM((CHUNKS, SIDE - 1, SIDE, BLOCK, LANES), bf16),
            pltpu.VMEM((CHUNKS, SIDE, SIDE, BLOCK, LANES), bf16),
            pltpu.VMEM((GRID * BLOCK, LANES), jnp.float32),
            pltpu.VMEM((CHUNKS, MEM // 2, 2, CHUNK, SHARE, LAT_PAD), bf16),
            dma((5,)), dma((len(PIECES),)), dma((len(PIECES),)), dma((CHUNKS,)), dma((CHUNKS,)), dma((CHUNKS,)),
            dma((len(PIECES),)), dma((CHUNKS,)), dma((CHUNKS,)), dma((CHUNKS,)), dma((1,)), dma((1,)), dma((1,)), dma((1,)), dma((1,)),
        ],
        compiler_params=pltpu.CompilerParams(collective_id=0, has_side_effects=True, vmem_limit_bytes=60 * 1024 * 1024),
    )(jnp.transpose(control, (0, 2, 1, 3)), jnp.transpose(perturbation, (0, 2, 1, 3)), vertical,
      lat_counts.reshape(1, GRID), lon_counts.reshape(1, GRID))
    return jnp.transpose(jnp.sum(shares.astype(jnp.float32), axis=0), (1, 0, 2))


def solution(mesh):
    in_specs = (P("mem", None, "grid", None), P("mem", None, "grid", None), P(), P(), P())
    out_specs = P("mem", "grid", None)
    return jax.shard_map(
        per_device, mesh=mesh, in_specs=in_specs, out_specs=out_specs, check_vma=False
    )
```
